32 devices in a mesh: grp: 2 (over x), tok: 16 (over z, y, core).
Axes of the slice: x: 2, y: 2, z: 4, core: 2. Of those that a mesh axis runs over, the one named last changes fastest.
Arguments:
- keys: bfloat16 [4096, 1024], P(('grp', 'tok')), parts along dimension 0, may hold values from -6 to 6
- values: bfloat16 [4096, 1024], P(('grp', 'tok')), parts along dimension 0, may hold values from -6 to 6
- queries: bfloat16 [4096, 1024], P(('grp', 'tok')), parts along dimension 0, may hold values from -6 to 6
- rates: float32 [2, 4096], P(None, ('grp', 'tok')), parts along dimension 1, may hold values from 0.3 to 3
- fast_weights: bfloat16 [2, 3, 512, 512], replicated, may hold values from -0.25 to 0.25
Outputs:
- readout: bfloat16 [4096, 1024], P(('grp', 'tok')), parts along dimension 0
- new_weights: bfloat16 [4, 3, 512, 512], P('grp'), parts along dimension 0
The draws below stay inside these ranges and needn't reach their ends.
There are 2 independent parts, one for each index of `grp`. The reference program is written for one: setup_inputs(seed, part) draws one part's arguments, and reference() takes and returns one part's arrays. A program takes and returns all parts, laid end to end along the dimension named above; an argument that names none is the same for every part. Nothing has to cross between parts.
All inputs are finite; a program needn't handle non-finite values.
Results may differ from the reference program's by a relative error of at most 0.017.
Values may be sent and summed in bfloat16 or wider, within the bound.
A program may use at most 64 MiB of HBM per device.

```python
import jax
import jax.numpy as jnp
from jax import lax

DH = 512
HEADS = 2
NS_STEPS = 2
GROUP = 2048


def draw_rates(key, part):
    ramp = 1.0 + 2.0 * jnp.arange(GROUP, dtype=jnp.float32) / (GROUP - 1)
    base = jnp.exp(jax.random.uniform(key, (HEADS, GROUP), jnp.float32, jnp.log(0.3), 0.0))
    return jnp.clip(base * ramp[None, :], 0.3, 3.0)


def levels(own_key, shape, shards, low, largest):
    factor_of = 1.0
    for axis_at, blocks in shards:
        draws = jax.random.uniform(jax.random.fold_in(jax.random.fold_in(own_key, 6), axis_at), (blocks,), jnp.float32, low / len(shards), largest / len(shards))
        factor_of = factor_of * jnp.repeat(jnp.exp(draws), shape[axis_at] // blocks).reshape((-1,) + (1,) * (len(shape) - 1 - axis_at))
    return factor_of


def scatter_about(stream_key, shape, scale, reach, cuts=(), held_as=jnp.bfloat16):
    values = jax.random.normal(stream_key, shape, jnp.float32) * scale
    if len(cuts) > 0:
        values = levels(stream_key, shape, cuts, -0.22, 0.18) * values
    return jnp.clip(values, min=-reach, max=reach).astype(held_as)


def setup_inputs(seed: int = 0, part: int = 0) -> dict:
    arg_keys = jax.random.split(jax.random.key(seed), 6)
    own_keys = jax.random.split(jax.random.fold_in(arg_keys[5], part), 6)
    return {
        "keys": scatter_about(own_keys[0], (GROUP, HEADS * DH), 1.0, 6.0, ((0, 16),)),
        "values": scatter_about(own_keys[1], (GROUP, HEADS * DH), 1.0, 6.0, ((0, 16),)),
        "queries": scatter_about(own_keys[2], (GROUP, HEADS * DH), 1.0, 6.0, ((0, 16),)),
        "rates": draw_rates(jax.random.fold_in(jax.random.fold_in(arg_keys[5], part), 71), part),
        "fast_weights": scatter_about(arg_keys[4], (HEADS, 3, DH, DH), DH ** -0.5, 0.25),
    }


def swiglu_grads(key_rows, value_rows, rate_col, gate_w, up_w, down_w):
    gate = jnp.dot(key_rows, gate_w, preferred_element_type=jnp.float32)
    upper = jnp.dot(key_rows, up_w, preferred_element_type=jnp.float32)
    sigma = jax.nn.sigmoid(gate)
    silu_gate = gate * sigma
    hidden = (silu_gate * upper).astype(jnp.bfloat16)
    outer = (-rate_col[:, None] * value_rows.astype(jnp.float32)).astype(jnp.bfloat16)
    back = jnp.dot(outer, down_w.T, preferred_element_type=jnp.float32)
    d_gate = (back * upper * sigma * (1.0 + gate * (1.0 - sigma))).astype(jnp.bfloat16)
    d_upper = (back * silu_gate).astype(jnp.bfloat16)
    grad_gate = jnp.dot(key_rows.T, d_gate, preferred_element_type=jnp.float32)
    grad_upper = jnp.dot(key_rows.T, d_upper, preferred_element_type=jnp.float32)
    grad_down = jnp.dot(hidden.T, outer, preferred_element_type=jnp.float32)
    return jnp.stack([grad_gate, grad_upper, grad_down])

def newton_schulz(matrix):
    wide = matrix.astype(jnp.float32)
    iterate = (wide / (jnp.sqrt(jnp.sum(wide * wide)) + 1e-07)).astype(jnp.bfloat16)
    for step in range(NS_STEPS):
        gram = jnp.dot(iterate, iterate.T, preferred_element_type=jnp.float32).astype(jnp.bfloat16)
        square = jnp.dot(gram, gram, preferred_element_type=jnp.float32)
        mixed = (-4.775 * gram.astype(jnp.float32) + 2.0315 * square).astype(jnp.bfloat16)
        iterate = (3.4445 * iterate.astype(jnp.float32) + jnp.dot(mixed, iterate, preferred_element_type=jnp.float32)).astype(jnp.bfloat16)
    return iterate

def renormed(weight, update):
    old = weight.astype(jnp.float32)
    fresh = old - update.astype(jnp.float32)
    scale = jnp.sqrt((lax.optimization_barrier(jnp.mean(old * old, axis=1, keepdims=True)) + 1e-06) / (lax.optimization_barrier(jnp.mean(fresh * fresh, axis=1, keepdims=True)) + 1e-06))
    return (fresh * scale).astype(jnp.bfloat16)

def apply_fast(query_rows, gate_w, up_w, down_w):
    gate = jnp.dot(query_rows, gate_w, preferred_element_type=jnp.float32)
    upper = jnp.dot(query_rows, up_w, preferred_element_type=jnp.float32)
    hidden = (jax.nn.silu(gate) * upper).astype(jnp.bfloat16)
    return jnp.dot(hidden, down_w, preferred_element_type=jnp.float32).astype(jnp.bfloat16)

def reference(keys, values, queries, rates, fast_weights):
    outputs = []
    weights_out = []
    for head in range(HEADS):
        cols = slice(head * DH, (head + 1) * DH)
        gate_w = fast_weights[head, 0]
        up_w = fast_weights[head, 1]
        down_w = fast_weights[head, 2]
        grads = swiglu_grads(keys[:, cols], values[:, cols], rates[head], gate_w, up_w, down_w)
        rounded = grads.astype(jnp.bfloat16)
        fresh = [renormed(fast_weights[head, which], newton_schulz(rounded[which])) for which in range(3)]
        weights_out.append(jnp.stack(fresh))
        outputs.append(apply_fast(queries[:, cols], fresh[0], fresh[1], fresh[2]))
    return (jnp.concatenate(outputs, axis=1), jnp.stack(weights_out))
```

```python
import functools

import jax
import jax.numpy as jnp
from jax import lax
from jax.experimental import pallas as pl
from jax.experimental.pallas import tpu as pltpu
from jax.sharding import PartitionSpec as P

HEADS = 2
NS_STEPS = 2
CHUNKS = 8
SUM_COLS = 256
SUM_ROWS = 128
PIECES = 2
SUM_LAG = 2
SUM_WAVE = 4
LAG = 4
WAVE = 4
BOTH = 4
SHIFT = 0
MESH = pl.DeviceIdType.MESH
F32 = jnp.float32
BF16 = jnp.bfloat16


def dot(a, b):
    return jnp.dot(a, b, preferred_element_type=F32)


def dot_nt(a, b):
    return lax.dot_general(a, b, (((1,), (1,)), ((), ())), preferred_element_type=F32)


def dot_tn(a, b):
    return lax.dot_general(a, b, (((0,), (0,)), ((), ())), preferred_element_type=F32)


def kernel(
    Z,
    k_hbm, v_hbm, q_hbm, r_hbm, w_hbm,
    out_ref, neww_ref,
    v_ref, q_ref, r_ref, w_ref,
    o_loc, keys, outer, grads, recv, sendbuf, part, m_buf, x_buf, g_buf, wn, hid,
    tok_send, tok_recv, chain_send, chain_recv, m_recv, w_send, w_recv, out_sem, in_sem,
):
    tokens = k_hbm.shape[0]
    D = w_ref.shape[1]
    half = D // 2
    R = D // CHUNKS
    SUM_CHUNKS = D * half // (SUM_ROWS * SUM_COLS)
    piece = tokens // PIECES
    me = lax.axis_index("tok")
    c = me % 2
    y = (me // 2) % 2
    z = me // 4

    def mid(h):
        return Z // 2 - 1 + SHIFT * h

    def at(zz, yy, cc):
        return {"tok": (zz * 2 + yy) * 2 + cc}

    def block_rows(p, j, n):
        return pl.ds(pl.multiple_of(p * tokens + j * n, n), n)

    def head_cols(h):
        return pl.ds(pl.multiple_of(h * D, D), D)

    sibling = at(z, y, 1 - c)
    across = at(z, 1 - y, c)
    mine = y * 2 + c
    other = (1 - y) * 2 + c
    half_cols = pl.ds(pl.multiple_of(c * half, half), half)

    loads = [
        pltpu.make_async_copy(src, dst, in_sem.at[n])
        for n, (src, dst) in enumerate((
            (r_hbm, r_ref), (v_hbm, v_ref),
            (k_hbm.at[:, head_cols(y)], keys.at[block_rows(mine, 0, tokens), :]),
            (w_hbm.at[y], w_ref), (q_hbm, q_ref),
        ))
    ]
    for load in loads:
        load.start()

    barrier = pltpu.get_barrier_semaphore()
    for peer in (sibling, across):
        pl.semaphore_signal(barrier, inc=1, device_id=peer, device_id_type=MESH)

    @pl.when(z > 0)
    def _():
        pl.semaphore_signal(barrier, inc=1, device_id={"tok": me - 4}, device_id_type=MESH)

    @pl.when(z < Z - 1)
    def _():
        pl.semaphore_signal(barrier, inc=1, device_id={"tok": me + 4}, device_id_type=MESH)

    loads[0].wait()
    loads[1].wait()
    for h in range(HEADS):
        row = jnp.broadcast_to(r_ref[h : h + 1, :], (128, tokens))
        col = jnp.concatenate([row.T] * (D // 128), axis=1)
        o_loc[h] = (-col * v_ref[:, h * D : (h + 1) * D].astype(F32)).astype(BF16)

    outer[block_rows(mine, 0, tokens), :] = o_loc[y]

    pl.semaphore_wait(barrier, 2 + jnp.where(z > 0, 1, 0) + jnp.where(z < Z - 1, 1, 0))

    def token_copy(a, j, kind):
        rows = slice(j * piece, (j + 1) * piece)
        held = (keys, outer)[a]
        if kind == 2:
            block = held.at[block_rows(other, j, piece), :]
            return pltpu.make_async_remote_copy(
                block, block, tok_send.at[a, kind, j], tok_recv.at[a, other, j],
                device_id=sibling, device_id_type=MESH)
        h = y if kind == 0 else 1 - y
        src = o_loc.at[h, rows, :] if a else k_hbm.at[rows, head_cols(h)]
        return pltpu.make_async_remote_copy(
            src, held.at[block_rows(mine, j, piece), :],
            tok_send.at[a, kind, j], tok_recv.at[a, mine, j],
            device_id=across if kind else sibling, device_id_type=MESH)

    for a in range(2):
        for kind in (1, 0):
            for j in range(PIECES):
                token_copy(a, j, kind).start()

    loads[2].wait()
    loads[3].wait()

    def forward_block(d, _):
        p = jnp.where(d < 2, y, 1 - y) * 2 + jnp.where(d % 2 == 0, c, 1 - c)

        @pl.when(d > 0)
        def _():
            for a in range(2):
                for j in range(PIECES):
                    block = (keys, outer)[a].at[block_rows(p, j, piece), :]
                    pltpu.make_async_remote_copy(
                        block, block, tok_send.at[a, 0, j], tok_recv.at[a, p, j],
                        device_id=sibling, device_id_type=MESH).wait_recv()

                    @pl.when(d == 2)
                    def _():
                        token_copy(a, j, 2).start()

        rows = block_rows(p, 0, tokens)
        key = keys[rows, :]
        gate = dot(key, w_ref[0, :, half_cols])
        upper = dot(key, w_ref[1, :, half_cols])
        back = dot_nt(outer[rows, :], w_ref[2, half_cols, :])
        sigma = jax.nn.sigmoid(gate)
        silu_gate = gate * sigma
        grads[2, rows, :] = (silu_gate * upper).astype(BF16)
        grads[0, rows, :] = (back * upper * sigma * (1.0 + gate * (1.0 - sigma))).astype(BF16)
        grads[1, rows, :] = (back * silu_gate).astype(BF16)
        return 0

    lax.fori_loop(0, 4, forward_block, 0)

    def owner_z(w, h):
        return (0, Z - 1, mid(h))[w]

    def owner_core(w, h):
        return h if w < 2 else 1 - h

    def chain_copy(w, i, step, side):
        return pltpu.make_async_remote_copy(
            sendbuf.at[w, i], recv.at[side, w, i],
            chain_send.at[w, i], chain_recv.at[side, w, i],
            device_id={"tok": me + step * 4}, device_id_type=MESH)

    def place(w, i):
        across_cols = (half if w < 2 else D) // SUM_COLS
        r = i // across_cols
        q = i % across_cols
        base_r = 0 if w < 2 else c * half
        base_q = c * half if w < 2 else 0
        return (
            pl.ds(pl.multiple_of(r * SUM_ROWS, SUM_ROWS), SUM_ROWS),
            pl.ds(pl.multiple_of(q * SUM_COLS, SUM_COLS), SUM_COLS),
            pl.ds(pl.multiple_of(base_r + r * SUM_ROWS, SUM_ROWS), SUM_ROWS),
            pl.ds(pl.multiple_of(base_q + q * SUM_COLS, SUM_COLS), SUM_COLS),
        )

    def hand_over(w, i):
        _, _, rows, cols = place(w, i)
        return pltpu.make_async_remote_copy(
            sendbuf.at[w, i], m_buf.at[rows, cols], chain_send.at[w, i], m_recv.at[i],
            device_id=sibling, device_id_type=MESH)

    def take(side, w, i):
        chain_copy(w, i, 1, side).wait_recv()
        part[...] += recv[side, w, i].astype(F32)

    def reduce_event(w, i):
        own = owner_z(w, y)
        keeps = jnp.logical_and(z == own, c == owner_core(w, y))
        left_cols, right_cols, rows, cols = place(w, i)
        if w < 2:
            part[...] = dot_tn(keys[:, left_cols], grads[w, :, right_cols])
        else:
            part[...] = dot_tn(grads[2, :, left_cols], outer[:, right_cols])

        @pl.when(jnp.logical_and(z > 0, z <= own))
        def _():
            take(0, w, i)

        @pl.when(jnp.logical_and(z < Z - 1, z >= own))
        def _():
            take(1, w, i)

        @pl.when(keeps)
        def _():
            m_buf[rows, cols] = part[...].astype(BF16)

        @pl.when(jnp.logical_not(keeps))
        def _():
            sendbuf[w, i] = part[...].astype(BF16)

        @pl.when(z < own)
        def _():
            chain_copy(w, i, 1, 0).start()

        @pl.when(z > own)
        def _():
            chain_copy(w, i, -1, 1).start()

        @pl.when(jnp.logical_and(z == own, jnp.logical_not(keeps)))
        def _():
            hand_over(w, i).start()

    def depth(w):
        own = owner_z(w, y)
        rise = jnp.where(z <= own, z, 0)
        fall = jnp.where(z >= own, Z - 1 - z, 0)
        return SUM_LAG * jnp.maximum(rise, fall) + (SUM_WAVE if w == 2 else 0)

    def reduce_step(t, _):
        for w in range(3):
            i = t - depth(w)

            @pl.when(jnp.logical_and(i >= 0, i < SUM_CHUNKS))
            def _():
                reduce_event(w, i)

        return 0

    lax.fori_loop(0, SUM_CHUNKS + SUM_WAVE + SUM_LAG * (Z - 1), reduce_step, 0)

    def stream_head(w):
        return c if w < 2 else 1 - c

    def owns(w):
        h = stream_head(w)
        return jnp.logical_and(y == h, z == owner_z(w, h))

    def w_copies(w, i, go):
        h = stream_head(w)
        own = owner_z(w, h)
        rows = pl.ds(pl.multiple_of(i * R, R), R)
        block = wn.at[h, w, rows, :]
        in_col = y == h
        both = i % BOTH == BOTH - 1
        along = jnp.logical_or(in_col, both)

        def copy(kind, dev):
            cp = pltpu.make_async_remote_copy(
                block, block, w_send.at[w, i, kind], w_recv.at[h, w, i],
                device_id=dev, device_id_type=MESH)
            cp.start() if go else cp.wait_send()

        @pl.when(jnp.logical_and(along, jnp.logical_and(z >= own, z < Z - 1)))
        def _():
            copy(0, {"tok": me + 4})

        @pl.when(jnp.logical_and(along, jnp.logical_and(z <= own, z > 0)))
        def _():
            copy(1, {"tok": me - 4})

        @pl.when(jnp.logical_and(in_col, jnp.logical_or(jnp.logical_not(both), z == own)))
        def _():
            copy(3, across)

        copy(2, sibling)

    def wait_block(h, w, i):
        rows = pl.ds(pl.multiple_of(i * R, R), R)
        block = wn.at[h, w, rows, :]
        pltpu.make_async_remote_copy(
            block, block, w_send.at[w, i, 2], w_recv.at[h, w, i],
            device_id=sibling, device_id_type=MESH).wait_recv()

    def renew(w):
        def gather(i, _):
            hand_over(w, i).wait_recv()
            return 0

        lax.fori_loop(0, SUM_CHUNKS, gather, 0)

    for w in range(3):

        @pl.when(owns(w))
        def _():
            renew(w)

    is_owner = functools.reduce(jnp.logical_or, [owns(w) for w in range(3)])
    owned_w = jnp.where(owns(0), 0, jnp.where(owns(1), 1, 2))

    @pl.when(is_owner)
    def _():
        wide = m_buf[...].astype(F32)
        norm = jnp.sqrt(jnp.sum(wide * wide)) + 1e-07
        m_buf[...] = (wide / norm).astype(BF16)
        for step in range(NS_STEPS):
            x = m_buf[...]
            g_buf[...] = dot_nt(x, x).astype(BF16)
            g = g_buf[...]
            mixed = (-4.775 * g.astype(F32) + 2.0315 * dot(g, g)).astype(BF16)
            x_buf[...] = 3.4445 * x.astype(F32) + dot(mixed, x)
            m_buf[...] = x_buf[...].astype(BF16)
        for i in range(CHUNKS):
            rows = slice(i * R, (i + 1) * R)
            old = w_ref[owned_w, rows, :].astype(F32)
            fresh = old - m_buf[rows, :].astype(F32)
            scale = jnp.sqrt(
                (jnp.mean(old * old, axis=1, keepdims=True) + 1e-06)
                / (jnp.mean(fresh * fresh, axis=1, keepdims=True) + 1e-06)
            )
            wn[y, owned_w, rows, :] = (fresh * scale).astype(BF16)
            for w in range(3):

                @pl.when(owned_w == w)
                def _():
                    w_copies(w, i, True)

    def spread(t, _):
        for w in range(3):
            h = stream_head(w)
            hops = jnp.abs(z - owner_z(w, h)) + jnp.where(y == h, 0, 1)
            i = t - LAG * (hops - 1) - (WAVE if w == 2 else 0)

            @pl.when(jnp.logical_and(hops > 0, jnp.logical_and(i >= 0, i < CHUNKS)))
            def _():
                wait_block(h, w, i)
                w_copies(w, i, True)

        return 0

    lax.fori_loop(0, CHUNKS + WAVE + LAG * (Z - 1), spread, 0)

    def save(h, w):
        return pltpu.make_async_copy(wn.at[h, w], neww_ref.at[h, w], out_sem.at[h, w])

    def wait_all(h, w):
        def one(i, _):
            wait_block(h, w, i)
            return 0

        lax.fori_loop(0, CHUNKS, one, 0)

    def hidden(h):
        query = q_ref[:, head_cols(h)]
        gate = dot(query, wn[h, 0])
        upper = dot(query, wn[h, 1])
        hid[h] = (gate * jax.nn.sigmoid(gate) * upper).astype(BF16)

    def finish(h):
        out_ref[:, head_cols(h)] = dot(hid[h], wn[h, 2]).astype(BF16)

    loads[4].wait()
    save(c, 0).start()
    save(c, 1).start()
    save(1 - c, 2).start()
    hidden(c)
    wait_all(1 - c, 0)
    save(1 - c, 0).start()
    wait_all(1 - c, 1)
    save(1 - c, 1).start()
    hidden(1 - c)
    finish(1 - c)
    wait_all(c, 2)
    save(c, 2).start()
    finish(c)

    for a in range(2):
        for kind in range(3):
            for j in range(PIECES):
                token_copy(a, j, kind).wait_send()

    def drain_sums(i, _):
        for w in range(3):
            own = owner_z(w, y)

            @pl.when(jnp.logical_not(jnp.logical_and(z == own, c == owner_core(w, y))))
            def _():
                chain_copy(w, i, 1, 0).wait_send()

        return 0

    lax.fori_loop(0, SUM_CHUNKS, drain_sums, 0)

    def drain(i, _):
        for w in range(3):
            w_copies(w, i, False)
        return 0

    lax.fori_loop(0, CHUNKS, drain, 0)
    for h in range(HEADS):
        for w in range(3):
            save(h, w).wait()


def store(a_ref, b_ref, a_out, b_out, sem):
    copies = [
        pltpu.make_async_copy(b_ref, b_out, sem.at[0]),
        pltpu.make_async_copy(a_ref, a_out, sem.at[1]),
    ]
    for cp in copies:
        cp.start()
    for cp in copies:
        cp.wait()


def body(Z, keys, values, queries, rates, fast_weights):
    D = fast_weights.shape[2]
    tokens = keys.shape[0]
    rows = tokens * 4
    sums = D * D // 2 // (SUM_ROWS * SUM_COLS)
    vmem = pl.BlockSpec(memory_space=pltpu.VMEM)
    hbm = pl.BlockSpec(memory_space=pltpu.MemorySpace.HBM)

    def run(*refs):
        kernel(Z, *refs)

    out, fresh = pl.pallas_call(
        run,
        out_shape=(
            jax.ShapeDtypeStruct((tokens, HEADS * D), BF16),
            jax.ShapeDtypeStruct((HEADS, 3, D, D), BF16),
        ),
        in_specs=[hbm] * 5,
        out_specs=(vmem, pl.BlockSpec(memory_space=pl.ANY)),
        scratch_shapes=[
            pltpu.VMEM((tokens, HEADS * D), BF16),
            pltpu.VMEM((tokens, HEADS * D), BF16),
            pltpu.VMEM(rates.shape, F32),
            pltpu.VMEM((3, D, D), BF16),
            pltpu.VMEM((HEADS, tokens, D), BF16),
            pltpu.VMEM((rows, D), BF16),
            pltpu.VMEM((rows, D), BF16),
            pltpu.VMEM((3, rows, D // 2), BF16),
            pltpu.VMEM((2, 3, sums, SUM_ROWS, SUM_COLS), BF16),
            pltpu.VMEM((3, sums, SUM_ROWS, SUM_COLS), BF16),
            pltpu.VMEM((SUM_ROWS, SUM_COLS), F32),
            pltpu.VMEM((D, D), BF16),
            pltpu.VMEM((D, D), F32),
            pltpu.VMEM((D, D), BF16),
            pltpu.VMEM((HEADS, 3, D, D), BF16),
            pltpu.VMEM((HEADS, tokens, D), BF16),
            pltpu.SemaphoreType.DMA((2, 3, PIECES)),
            pltpu.SemaphoreType.DMA((2, 4, PIECES)),
            pltpu.SemaphoreType.DMA((3, sums)),
            pltpu.SemaphoreType.DMA((2, 3, sums)),
            pltpu.SemaphoreType.DMA((sums,)),
            pltpu.SemaphoreType.DMA((3, CHUNKS, 4)),
            pltpu.SemaphoreType.DMA((HEADS, 3, CHUNKS)),
            pltpu.SemaphoreType.DMA((HEADS, 3)),
            pltpu.SemaphoreType.DMA((5,)),
        ],
        compiler_params=pltpu.CompilerParams(
            collective_id=0, has_side_effects=True, vmem_limit_bytes=30 * 1024 * 1024
        ),
        name="ttt_step",
    )(*[pltpu.with_memory_space_constraint(a, pltpu.MemorySpace.HBM) for a in (keys, values, queries, rates, fast_weights)])
    anywhere = pl.BlockSpec(memory_space=pl.ANY)
    return pl.pallas_call(
        store,
        out_shape=(
            jax.ShapeDtypeStruct(out.shape, BF16),
            jax.ShapeDtypeStruct(fresh.shape, BF16),
        ),
        in_specs=[anywhere] * 2,
        out_specs=(hbm, hbm),
        scratch_shapes=[pltpu.SemaphoreType.DMA((2,))],
        compiler_params=pltpu.CompilerParams(vmem_limit_bytes=1024 * 1024),
        name="store",
    )(out, fresh)


def solution(mesh):
    Z = mesh.shape["tok"] // 4
    return jax.shard_map(
        functools.partial(body, Z),
        mesh=mesh,
        in_specs=(
            P(("grp", "tok"), None),
            P(("grp", "tok"), None),
            P(("grp", "tok"), None),
            P(None, ("grp", "tok")),
            P(),
        ),
        out_specs=(P(("grp", "tok"), None), P("grp", None, None, None)),
        check_vma=False,
    )
```

```python
import functools

import jax
import jax.numpy as jnp
from jax import lax
from jax.experimental import pallas as pl
from jax.experimental.pallas import tpu as pltpu
from jax.sharding import PartitionSpec as P

HEADS = 2
NS_STEPS = 2
CHUNKS = 8
SUM_COLS = 256
SUM_ROWS = 128
SUM_LAG = 6
LAG = 4
WAVE = 4
LEAF = 12
SHIFT = 0
MESH = pl.DeviceIdType.MESH
F32 = jnp.float32
BF16 = jnp.bfloat16


def dot(a, b):
    return jnp.dot(a, b, preferred_element_type=F32)


def dot_nt(a, b):
    return lax.dot_general(a, b, (((1,), (1,)), ((), ())), preferred_element_type=F32)


def dot_tn(a, b):
    return lax.dot_general(a, b, (((0,), (0,)), ((), ())), preferred_element_type=F32)


def kernel(
    Z,
    k_hbm, v_hbm, q_hbm, r_hbm, w_hbm,
    query_ref, neww_ref,
    v_ref, r_ref, w_ref,
    o_loc, keys, outer, gates, grads, recv, sendbuf, part, m_buf, x_buf, g_buf, wn,
    tok_send, tok_recv, chain_send, chain_recv, w_send, w_recv, s_recv, out_sem, in_sem, clear,
):
    tokens = k_hbm.shape[0]
    D = w_ref.shape[1]
    R = D // CHUNKS
    SUM_CHUNKS = D * D // (SUM_ROWS * SUM_COLS)
    me = lax.axis_index("tok")
    c = me % 2
    y = (me // 2) % 2
    z = me // 4

    def mid(h):
        return Z // 2 - 1 + SHIFT * h

    def at(zz, yy, cc):
        return {"tok": (zz * 2 + yy) * 2 + cc}

    def block_rows(p):
        return pl.ds(pl.multiple_of(p * tokens, tokens), tokens)

    def head_cols(h):
        return pl.ds(pl.multiple_of(h * D, D), D)

    sibling = at(z, y, 1 - c)
    across = at(z, 1 - y, c)
    mine = y * 2 + c
    pair = c == y
    gatherer = at(z, 1 - y, 1 - y)

    barrier = pltpu.get_barrier_semaphore()
    for peer in (sibling, across, at(z, 1 - y, 1 - c)):
        pl.semaphore_signal(barrier, inc=1, device_id=peer, device_id_type=MESH)

    @pl.when(z > 0)
    def _():
        pl.semaphore_signal(barrier, inc=1, device_id={"tok": me - 4}, device_id_type=MESH)

    @pl.when(z < Z - 1)
    def _():
        pl.semaphore_signal(barrier, inc=1, device_id={"tok": me + 4}, device_id_type=MESH)

    loads = [
        pltpu.make_async_copy(src, dst, in_sem.at[n])
        for n, (src, dst) in enumerate((
            (r_hbm, r_ref), (v_hbm, v_ref),
            (k_hbm.at[:, head_cols(y)], keys.at[block_rows(mine), :]),
            (w_hbm.at[y], w_ref), (q_hbm, query_ref),
        ))
    ]
    for load in loads:
        load.start()

    loads[0].wait()
    loads[1].wait()
    for h in range(HEADS):
        row = jnp.broadcast_to(r_ref[h : h + 1, :], (128, tokens))
        col = jnp.concatenate([row.T] * (D // 128), axis=1)
        o_loc[h] = (-col * v_ref[:, h * D : (h + 1) * D].astype(F32)).astype(BF16)

    outer[block_rows(mine), :] = o_loc[y]

    pl.semaphore_wait(barrier, 3 + jnp.where(z > 0, 1, 0) + jnp.where(z < Z - 1, 1, 0))

    def token_copy(a, kind):
        h = y if kind == 0 else 1 - y
        src = o_loc.at[h] if a else k_hbm.at[:, head_cols(h)]
        return pltpu.make_async_remote_copy(
            src, (keys, outer)[a].at[block_rows(mine), :],
            tok_send.at[kind], tok_recv.at[a, mine],
            device_id=gatherer if kind else sibling, device_id_type=MESH)

    def pass_on(a, p):
        block = (keys, outer)[a].at[block_rows(p), :]
        return pltpu.make_async_remote_copy(
            block, block, tok_send.at[2], tok_recv.at[a, p],
            device_id=sibling, device_id_type=MESH)

    def token_wait(kind):
        block = keys.at[pl.ds(0, tokens * (4 if kind == 2 else 2)), :]
        return pltpu.make_async_remote_copy(
            block, block, tok_send.at[kind], tok_recv.at[0, 0],
            device_id=sibling, device_id_type=MESH)

    for a in range(2):
        for kind in (1, 0):
            token_copy(a, kind).start()

    loads[2].wait()
    loads[3].wait()

    def forward_step(s, _):
        d = s // 4 * 2 + s % 2
        p = jnp.where(d < 2, y * 2 + jnp.where(d == 0, c, 1 - c), (1 - y) * 2 + d % 2)
        rows = block_rows(p)
        for a in range(2):

            @pl.when(jnp.logical_and(s // 2 % 2 == a, d > 0))
            def _():
                pass_on(a, p).wait_recv()

                @pl.when(jnp.logical_and(pair, d >= 2))
                def _():
                    pass_on(a, p).start()

        @pl.when(s // 2 % 2 == 0)
        def _():
            key = keys[rows, :]
            gate = dot(key, w_ref[0])
            upper = dot(key, w_ref[1])

            @pl.when(pair)
            def _():
                gates[0, rows, :] = gate
                gates[1, rows, :] = upper

            @pl.when(jnp.logical_not(pair))
            def _():
                grads[0, rows, :] = (gate * jax.nn.sigmoid(gate) * upper).astype(BF16)

        @pl.when(jnp.logical_and(pair, s // 2 % 2 == 1))
        def _():
            gate = gates[0, rows, :]
            upper = gates[1, rows, :]
            back = dot_nt(outer[rows, :], w_ref[2])
            sigma = jax.nn.sigmoid(gate)
            grads[0, rows, :] = (back * upper * sigma * (1.0 + gate * (1.0 - sigma))).astype(BF16)
            grads[1, rows, :] = (back * (gate * sigma)).astype(BF16)

        return 0

    lax.fori_loop(0, 8, forward_step, 0)

    def owner_z(w, h):
        return (0, Z - 1, mid(h))[w]

    def slot(w, side=0):
        return w if w < 2 else side

    def chain_copy(w, i, step, side):
        late = jnp.where(i == SUM_CHUNKS - 1, 1, 0)
        return pltpu.make_async_remote_copy(
            sendbuf.at[slot(w), i], recv.at[slot(w, side), i],
            chain_send.at[slot(w), late], chain_recv.at[slot(w, side), i],
            device_id={"tok": me + step * 4}, device_id_type=MESH)

    def chain_sent(w, late):
        block = sendbuf.at[slot(w), pl.ds((SUM_CHUNKS - 1) * late, 1 if late else SUM_CHUNKS - 1)]
        return pltpu.make_async_remote_copy(
            block, block, chain_send.at[slot(w), late], chain_recv.at[slot(w), 0],
            device_id=sibling, device_id_type=MESH)

    def place(i):
        across_cols = D // SUM_COLS
        r = i // across_cols
        q = i % across_cols
        return (
            pl.ds(pl.multiple_of(r * SUM_ROWS, SUM_ROWS), SUM_ROWS),
            pl.ds(pl.multiple_of(q * SUM_COLS, SUM_COLS), SUM_COLS),
        )

    def take(side, w, i):
        chain_copy(w, i, 1, side).wait_recv()
        part[...] += recv[slot(w, side), i].astype(F32)

    def starts(w):
        own = owner_z(w, y)
        return jnp.logical_or(
            jnp.logical_and(z == 0, own != 0), jnp.logical_and(z == Z - 1, own != Z - 1)
        )

    def reduce_event(w, i):
        own = owner_z(w, y)
        rows, cols = place(i)
        if w < 2:
            part[...] = dot_tn(keys[:, rows], grads[w, :, cols])
        else:
            part[...] = dot_tn(grads[0, :, rows], outer[:, cols])

        @pl.when(jnp.logical_and(z > 0, z <= own))
        def _():
            take(0, w, i)

        @pl.when(jnp.logical_and(z < Z - 1, z >= own))
        def _():
            take(1, w, i)

        @pl.when(z == own)
        def _():
            m_buf[rows, cols] = part[...].astype(BF16)

        @pl.when(z != own)
        def _():
            sendbuf[slot(w), i] = part[...].astype(BF16)

        if w == 2:

            @pl.when(jnp.logical_and(starts(w), i == 0))
            def _():
                pl.semaphore_wait(clear, 1)

        @pl.when(z < own)
        def _():
            chain_copy(w, i, 1, 0).start()

        @pl.when(z > own)
        def _():
            chain_copy(w, i, -1, 1).start()

    def depth(w):
        own = owner_z(w, y)
        rise = jnp.where(z <= own, z, 0)
        fall = jnp.where(z >= own, Z - 1 - z, 0)
        return SUM_LAG * jnp.maximum(rise, fall)

    def reduce_step(t, _):
        for w in range(3):
            i = t - depth(w)

            @pl.when(jnp.logical_and(pair == (w < 2), jnp.logical_and(i >= 0, i < SUM_CHUNKS)))
            def _():
                reduce_event(w, i)

        for w in range(2):

            @pl.when(jnp.logical_and(pair, jnp.logical_and(starts(w), t == SUM_CHUNKS - 1)))
            def _():
                chain_sent(w, 0).wait_send()
                pl.semaphore_signal(clear, inc=1, device_id=sibling, device_id_type=MESH)

        return 0

    lax.fori_loop(0, SUM_CHUNKS + SUM_LAG * (Z - 1), reduce_step, 0)

    def stream_head(w):
        return c if w < 2 else 1 - c

    def owns(w):
        h = stream_head(w)
        return jnp.logical_and(y == h, z == owner_z(w, h))

    def w_copies(w, i):
        h = stream_head(w)
        rows = pl.ds(pl.multiple_of(i * R, R), R)
        block = wn.at[h, w, rows, :]

        def copy(kind, dev):
            done = s_recv.at[w] if kind == 2 else w_recv.at[w, i]
            pltpu.make_async_remote_copy(
                block, block, w_send.at[w, kind], done,
                device_id=dev, device_id_type=MESH).start()

        for kind, go, dev in w_targets(w):

            @pl.when(go)
            def _():
                copy(kind, dev)

    def w_targets(w):
        h = stream_head(w)
        own = owner_z(w, h)
        in_col = y == h
        return (
            (0, jnp.logical_and(in_col, jnp.logical_and(z >= own, z < Z - 1)), {"tok": me + 4}),
            (1, jnp.logical_and(in_col, jnp.logical_and(z <= own, z > 0)), {"tok": me - 4}),
            (3, in_col, across),
            (2, z >= 0, sibling),
        )

    def w_wait(h, w, block, send, done):
        return pltpu.make_async_remote_copy(
            block, block, send, done, device_id=sibling, device_id_type=MESH)

    def wait_block(h, w, i):
        rows = pl.ds(pl.multiple_of(i * R, R), R)
        block = wn.at[h, w, rows, :]
        w_wait(h, w, block, w_send.at[w, 2], w_recv.at[w, i]).wait_recv()

    is_owner = functools.reduce(jnp.logical_or, [owns(w) for w in range(3)])
    owned_w = jnp.where(owns(0), 0, jnp.where(owns(1), 1, 2))

    @pl.when(is_owner)
    def _():
        wide = m_buf[...].astype(F32)
        norm = jnp.sqrt(jnp.sum(wide * wide)) + 1e-07
        m_buf[...] = (wide / norm).astype(BF16)
        for step in range(NS_STEPS):
            x = m_buf[...]
            g_buf[...] = dot_nt(x, x).astype(BF16)
            g = g_buf[...]
            mixed = (-4.775 * g.astype(F32) + 2.0315 * dot(g, g)).astype(BF16)
            x_buf[...] = 3.4445 * x.astype(F32) + dot(mixed, x)
            m_buf[...] = x_buf[...].astype(BF16)
        for i in range(CHUNKS):
            rows = slice(i * R, (i + 1) * R)
            old = w_ref[owned_w, rows, :].astype(F32)
            fresh = old - m_buf[rows, :].astype(F32)
            scale = jnp.sqrt(
                (jnp.mean(old * old, axis=1, keepdims=True) + 1e-06)
                / (jnp.mean(fresh * fresh, axis=1, keepdims=True) + 1e-06)
            )
            wn[y, owned_w, rows, :] = (fresh * scale).astype(BF16)
            for w in range(3):

                @pl.when(owned_w == w)
                def _():
                    w_copies(w, i)

    def spread(t, _):
        for w in range(3):
            h = stream_head(w)
            own = owner_z(w, h)
            hops = jnp.abs(z - own) + jnp.where(y == h, 0, 1)
            shared = (jnp.logical_and(z > mid(h), w == 0), jnp.logical_and(z < mid(h), w == 1), False)[w]
            stride = jnp.where(shared, 2, 1)
            u = t - LAG * (hops - 1) - (WAVE if w == 2 else 0) - jnp.where(y == h, 0, LEAF)
            i = jnp.where(shared, (u + 16) // 2 - 8, u)

            @pl.when(jnp.logical_and(
                jnp.logical_and(hops > 0, jnp.logical_or(jnp.logical_not(shared), u % 2 == 0)),
                jnp.logical_and(u >= 0, i < CHUNKS)))
            def _():
                wait_block(h, w, i)
                w_copies(w, i)

        return 0

    lax.fori_loop(0, 2 * CHUNKS + WAVE + LEAF + LAG * (Z - 1), spread, 0)

    def save(h, w):
        return pltpu.make_async_copy(wn.at[h, w], neww_ref.at[h, w], out_sem.at[0])

    def finish(w):
        h = 1 - stream_head(w)
        w_wait(h, w, wn.at[h, w], w_send.at[w, 2], s_recv.at[w]).wait_recv()
        save(h, w).start()

    for w in range(3):
        save(stream_head(w), w).start()
    for w in range(3):
        finish(w)
    loads[4].wait()

    for kind in range(2):
        token_wait(kind).wait_send()

    @pl.when(pair)
    def _():
        token_wait(2).wait_send()

    for w in range(3):
        moved = jnp.logical_and(pair == (w < 2), z != owner_z(w, y))

        @pl.when(jnp.logical_and(moved, jnp.logical_not(starts(w))) if w < 2 else moved)
        def _():
            chain_sent(w, 0).wait_send()

        @pl.when(moved)
        def _():
            chain_sent(w, 1).wait_send()

        for kind, go, _ in w_targets(w):

            @pl.when(go)
            def _():
                w_wait(0, w, wn.at[stream_head(w), w], w_send.at[w, kind], s_recv.at[w]).wait_send()

    pltpu.make_async_copy(wn, neww_ref, out_sem.at[0]).wait()


def readout(query_ref, w_ref, out, w_out, out_v, sem):
    copies = [
        pltpu.make_async_copy(w_ref, w_out, sem.at[0]),
        pltpu.make_async_copy(out_v, out, sem.at[1]),
    ]
    copies[0].start()
    D = w_ref.shape[2]
    for h in range(HEADS):
        cols = slice(h * D, (h + 1) * D)
        query = query_ref[:, cols]
        gate = dot(query, w_ref[h, 0])
        upper = dot(query, w_ref[h, 1])
        hidden = (gate * jax.nn.sigmoid(gate) * upper).astype(BF16)
        out_v[:, cols] = dot(hidden, w_ref[h, 2]).astype(BF16)
    copies[1].start()
    for cp in copies:
        cp.wait()


def body(Z, keys, values, queries, rates, fast_weights):
    D = fast_weights.shape[2]
    tokens = keys.shape[0]
    rows = tokens * 4
    sums = D * D // (SUM_ROWS * SUM_COLS)
    vmem = pl.BlockSpec(memory_space=pltpu.VMEM)
    hbm = pl.BlockSpec(memory_space=pltpu.MemorySpace.HBM)

    def run(*refs):
        kernel(Z, *refs)

    query, fresh = pl.pallas_call(
        run,
        out_shape=(
            jax.ShapeDtypeStruct((tokens, HEADS * D), BF16),
            jax.ShapeDtypeStruct((HEADS, 3, D, D), BF16),
        ),
        in_specs=[hbm] * 5,
        out_specs=(pl.BlockSpec(memory_space=pl.ANY), pl.BlockSpec(memory_space=pl.ANY)),
        scratch_shapes=[
            pltpu.VMEM((tokens, HEADS * D), BF16),
            pltpu.VMEM(rates.shape, F32),
            pltpu.VMEM((3, D, D), BF16),
            pltpu.VMEM((HEADS, tokens, D), BF16),
            pltpu.VMEM((rows, D), BF16),
            pltpu.VMEM((rows, D), BF16),
            pltpu.VMEM((2, rows, D), F32),
            pltpu.VMEM((2, rows, D), BF16),
            pltpu.VMEM((2, sums, SUM_ROWS, SUM_COLS), BF16),
            pltpu.VMEM((2, sums, SUM_ROWS, SUM_COLS), BF16),
            pltpu.VMEM((SUM_ROWS, SUM_COLS), F32),
            pltpu.VMEM((D, D), BF16),
            pltpu.VMEM((D, D), F32),
            pltpu.VMEM((D, D), BF16),
            pltpu.VMEM((HEADS, 3, D, D), BF16),
            pltpu.SemaphoreType.DMA((3,)),
            pltpu.SemaphoreType.DMA((2, 4)),
            pltpu.SemaphoreType.DMA((2, 2)),
            pltpu.SemaphoreType.DMA((2, sums)),
            pltpu.SemaphoreType.DMA((3, 4)),
            pltpu.SemaphoreType.DMA((3, CHUNKS)),
            pltpu.SemaphoreType.DMA((3,)),
            pltpu.SemaphoreType.DMA((1,)),
            pltpu.SemaphoreType.DMA((5,)),
            pltpu.SemaphoreType.REGULAR,
        ],
        compiler_params=pltpu.CompilerParams(
            collective_id=0, has_side_effects=True, vmem_limit_bytes=30 * 1024 * 1024
        ),
        name="ttt_step",
    )(*[pltpu.with_memory_space_constraint(a, pltpu.MemorySpace.HBM) for a in (keys, values, queries, rates, fast_weights)])
    return pl.pallas_call(
        readout,
        out_shape=(
            jax.ShapeDtypeStruct(query.shape, BF16),
            jax.ShapeDtypeStruct(fresh.shape, BF16),
        ),
        in_specs=[vmem] * 2,
        out_specs=(hbm, hbm),
        scratch_shapes=[
            pltpu.VMEM(query.shape, BF16),
            pltpu.SemaphoreType.DMA((2,)),
        ],
        compiler_params=pltpu.CompilerParams(vmem_limit_bytes=4 * 1024 * 1024),
        name="readout",
    )(query, fresh)


def solution(mesh):
    Z = mesh.shape["tok"] // 4
    return jax.shard_map(
        functools.partial(body, Z),
        mesh=mesh,
        in_specs=(
            P(("grp", "tok"), None),
            P(("grp", "tok"), None),
            P(("grp", "tok"), None),
            P(None, ("grp", "tok")),
            P(),
        ),
        out_specs=(P(("grp", "tok"), None), P("grp", None, None, None)),
        check_vma=False,
    )
```

```python
import functools

import jax
import jax.numpy as jnp
from jax import lax
from jax.experimental import pallas as pl
from jax.experimental.pallas import tpu as pltpu
from jax.sharding import PartitionSpec as P

HEADS = 2
NS_STEPS = 2
CHUNKS = 8
SUM_COLS = 256
SUM_ROWS = 128
SUM_LAG = 4
LAG = 4
LEAF = 12
SHIFT = 0
MESH = pl.DeviceIdType.MESH
F32 = jnp.float32
BF16 = jnp.bfloat16


def dot(a, b):
    return jnp.dot(a, b, preferred_element_type=F32)


def dot_nt(a, b):
    return lax.dot_general(a, b, (((1,), (1,)), ((), ())), preferred_element_type=F32)


def dot_tn(a, b):
    return lax.dot_general(a, b, (((0,), (0,)), ((), ())), preferred_element_type=F32)


def kernel(
    Z,
    k_hbm, v_hbm, q_hbm, r_hbm, w_hbm,
    query_ref, neww_ref,
    v_ref, r_ref, w_ref,
    o_loc, keys, outer, gates, grads, recv, sendbuf, part, m_buf, x_buf, g_buf, wn,
    tok_send, tok_recv, chain_send, chain_recv, w_send, w_recv, s_recv, out_sem, in_sem, clear,
):
    tokens = k_hbm.shape[0]
    D = w_ref.shape[1]
    R = D // CHUNKS
    SUM_CHUNKS = D * D // (SUM_ROWS * SUM_COLS)
    me = lax.axis_index("tok")
    c = me % 2
    y = (me // 2) % 2
    z = me // 4

    def mid(h):
        return Z // 2 - 1 + SHIFT * h

    def at(zz, yy, cc):
        return {"tok": (zz * 2 + yy) * 2 + cc}

    def block_rows(p):
        return pl.ds(pl.multiple_of(p * tokens, tokens), tokens)

    def head_cols(h):
        return pl.ds(pl.multiple_of(h * D, D), D)

    sibling = at(z, y, 1 - c)
    across = at(z, 1 - y, c)
    mine = y * 2 + c
    pair = c == 1
    gatherer = at(z, 1 - y, 1)

    barrier = pltpu.get_barrier_semaphore()
    for peer in (sibling, across, at(z, 1 - y, 1 - c)):
        pl.semaphore_signal(barrier, inc=1, device_id=peer, device_id_type=MESH)

    @pl.when(z > 0)
    def _():
        pl.semaphore_signal(barrier, inc=1, device_id={"tok": me - 4}, device_id_type=MESH)

    @pl.when(z < Z - 1)
    def _():
        pl.semaphore_signal(barrier, inc=1, device_id={"tok": me + 4}, device_id_type=MESH)

    loads = [
        pltpu.make_async_copy(src, dst, in_sem.at[n])
        for n, (src, dst) in enumerate((
            (r_hbm, r_ref), (v_hbm, v_ref),
            (k_hbm.at[:, head_cols(y)], keys.at[block_rows(mine), :]),
            (w_hbm.at[y], w_ref), (q_hbm, query_ref),
        ))
    ]
    for load in loads:
        load.start()

    loads[0].wait()
    loads[1].wait()
    for h in range(HEADS):
        row = jnp.broadcast_to(r_ref[h : h + 1, :], (128, tokens))
        col = jnp.concatenate([row.T] * (D // 128), axis=1)
        o_loc[h] = (-col * v_ref[:, h * D : (h + 1) * D].astype(F32)).astype(BF16)

    outer[block_rows(mine), :] = o_loc[y]

    pl.semaphore_wait(barrier, 3 + jnp.where(z > 0, 1, 0) + jnp.where(z < Z - 1, 1, 0))

    def token_copy(a, kind):
        h = y if kind == 0 else 1 - y
        src = o_loc.at[h] if a else k_hbm.at[:, head_cols(h)]
        return pltpu.make_async_remote_copy(
            src, (keys, outer)[a].at[block_rows(mine), :],
            tok_send.at[kind], tok_recv.at[a, mine],
            device_id=gatherer if kind else sibling, device_id_type=MESH)

    def pass_on(a, p):
        block = (keys, outer)[a].at[block_rows(p), :]
        return pltpu.make_async_remote_copy(
            block, block, tok_send.at[2], tok_recv.at[a, p],
            device_id=sibling, device_id_type=MESH)

    def token_wait(kind):
        block = keys.at[pl.ds(0, tokens * (4 if kind == 2 else 2)), :]
        return pltpu.make_async_remote_copy(
            block, block, tok_send.at[kind], tok_recv.at[0, 0],
            device_id=sibling, device_id_type=MESH)

    for a in range(2):
        for kind in (1, 0):
            token_copy(a, kind).start()

    loads[2].wait()
    loads[3].wait()

    def forward_step(s, _):
        d = s // 4 * 2 + s % 2
        p = jnp.where(d < 2, y * 2 + jnp.where(d == 0, c, 1 - c), (1 - y) * 2 + d % 2)
        rows = block_rows(p)
        for a in range(2):

            @pl.when(jnp.logical_and(s // 2 % 2 == a, d > 0))
            def _():
                pass_on(a, p).wait_recv()

                @pl.when(jnp.logical_and(pair, d >= 2))
                def _():
                    pass_on(a, p).start()

        @pl.when(s // 2 % 2 == 0)
        def _():
            key = keys[rows, :]
            gate = dot(key, w_ref[0])
            upper = dot(key, w_ref[1])

            @pl.when(pair)
            def _():
                gates[0, rows, :] = gate
                gates[1, rows, :] = upper

            @pl.when(jnp.logical_not(pair))
            def _():
                grads[0, rows, :] = (gate * jax.nn.sigmoid(gate) * upper).astype(BF16)

        @pl.when(jnp.logical_and(pair, s // 2 % 2 == 1))
        def _():
            gate = gates[0, rows, :]
            upper = gates[1, rows, :]
            back = dot_nt(outer[rows, :], w_ref[2])
            sigma = jax.nn.sigmoid(gate)
            grads[0, rows, :] = (back * upper * sigma * (1.0 + gate * (1.0 - sigma))).astype(BF16)
            grads[1, rows, :] = (back * (gate * sigma)).astype(BF16)

        return 0

    lax.fori_loop(0, 8, forward_step, 0)

    def owner_z(w, h):
        return (0, Z - 1, mid(h))[w]

    def slot(w, side=0):
        return w if w < 2 else side

    def chain_copy(w, i, step, side):
        late = jnp.where(i == SUM_CHUNKS - 1, 1, 0)
        return pltpu.make_async_remote_copy(
            sendbuf.at[slot(w), i], recv.at[slot(w, side), i],
            chain_send.at[slot(w), late], chain_recv.at[slot(w, side), i],
            device_id={"tok": me + step * 4}, device_id_type=MESH)

    def chain_sent(w, late):
        block = sendbuf.at[slot(w), pl.ds((SUM_CHUNKS - 1) * late, 1 if late else SUM_CHUNKS - 1)]
        return pltpu.make_async_remote_copy(
            block, block, chain_send.at[slot(w), late], chain_recv.at[slot(w), 0],
            device_id=sibling, device_id_type=MESH)

    def place(i):
        across_cols = D // SUM_COLS
        r = i // across_cols
        q = i % across_cols
        return (
            pl.ds(pl.multiple_of(r * SUM_ROWS, SUM_ROWS), SUM_ROWS),
            pl.ds(pl.multiple_of(q * SUM_COLS, SUM_COLS), SUM_COLS),
        )

    def take(side, w, i):
        chain_copy(w, i, 1, side).wait_recv()
        part[...] += recv[slot(w, side), i].astype(F32)

    def starts(w):
        own = owner_z(w, y)
        return jnp.logical_or(
            jnp.logical_and(z == 0, own != 0), jnp.logical_and(z == Z - 1, own != Z - 1)
        )

    def reduce_event(w, i):
        own = owner_z(w, y)
        rows, cols = place(i)
        if w < 2:
            part[...] = dot_tn(keys[:, rows], grads[w, :, cols])
        else:
            part[...] = dot_tn(grads[0, :, rows], outer[:, cols])

        @pl.when(jnp.logical_and(z > 0, z <= own))
        def _():
            take(0, w, i)

        @pl.when(jnp.logical_and(z < Z - 1, z >= own))
        def _():
            take(1, w, i)

        @pl.when(z == own)
        def _():
            m_buf[rows, cols] = part[...].astype(BF16)

        @pl.when(z != own)
        def _():
            sendbuf[slot(w), i] = part[...].astype(BF16)

        if w == 2:

            @pl.when(jnp.logical_and(starts(w), i == 0))
            def _():
                pl.semaphore_wait(clear, 1)

        @pl.when(z < own)
        def _():
            chain_copy(w, i, 1, 0).start()

        @pl.when(z > own)
        def _():
            chain_copy(w, i, -1, 1).start()

    def depth(w):
        own = owner_z(w, y)
        rise = jnp.where(z <= own, z, 0)
        fall = jnp.where(z >= own, Z - 1 - z, 0)
        return SUM_LAG * jnp.maximum(rise, fall)

    def reduce_all(ws):
        depths = [depth(w) for w in ws]
        first = [starts(w) for w in ws]

        def step(t, _):
            for w, lag in zip(ws, depths):
                i = t - lag

                @pl.when(jnp.logical_and(i >= 0, i < SUM_CHUNKS))
                def _():
                    reduce_event(w, i)

            if len(ws) == 2:
                for w, head in zip(ws, first):

                    @pl.when(jnp.logical_and(head, t == SUM_CHUNKS - 1))
                    def _():
                        chain_sent(w, 0).wait_send()
                        pl.semaphore_signal(clear, inc=1, device_id=sibling, device_id_type=MESH)

            return 0

        lax.fori_loop(0, SUM_CHUNKS + functools.reduce(jnp.maximum, depths), step, 0)

    @pl.when(pair)
    def _():
        reduce_all((0, 1))

    @pl.when(jnp.logical_not(pair))
    def _():
        reduce_all((2,))

    def owns(w):
        return jnp.logical_and(pair == (w < 2), z == owner_z(w, y))

    def stream(h, w):
        return h * 2 + w % 2

    def w_targets(w, home):
        own = owner_z(w, y)
        leaf = (2, True, sibling)
        if not home:
            return (leaf,)
        return (
            (0, jnp.logical_and(z >= own, z < Z - 1), {"tok": me + 4}),
            (1, jnp.logical_and(z <= own, z > 0), {"tok": me - 4}),
            (3, True, across),
            leaf,
        )

    def w_copies(h, w, i, targets):
        rows = pl.ds(pl.multiple_of(i * R, R), R)
        block = wn.at[h, w, rows, :]
        n = stream(h, w)

        def copy(kind, dev):
            pltpu.make_async_remote_copy(
                block, block, w_send.at[n, kind], s_recv.at[n] if kind == 2 else w_recv.at[n, i],
                device_id=dev, device_id_type=MESH).start()

        for kind, go, dev in targets:
            if go is True:
                copy(kind, dev)
            else:

                @pl.when(go)
                def _():
                    copy(kind, dev)

    def w_wait(h, w, kind):
        block = wn.at[h, w]
        n = stream(h, w)
        return pltpu.make_async_remote_copy(
            block, block, w_send.at[n, kind], s_recv.at[n],
            device_id=sibling, device_id_type=MESH)

    def wait_block(h, w, i):
        rows = pl.ds(pl.multiple_of(i * R, R), R)
        block = wn.at[h, w, rows, :]
        n = stream(h, w)
        pltpu.make_async_remote_copy(
            block, block, w_send.at[n, 2], w_recv.at[n, i],
            device_id=sibling, device_id_type=MESH).wait_recv()

    is_owner = functools.reduce(jnp.logical_or, [owns(w) for w in range(3)])
    owned_w = jnp.where(owns(0), 0, jnp.where(owns(1), 1, 2))

    @pl.when(is_owner)
    def _():
        wide = m_buf[...].astype(F32)
        norm = jnp.sqrt(jnp.sum(wide * wide)) + 1e-07
        m_buf[...] = (wide / norm).astype(BF16)
        for step in range(NS_STEPS):
            x = m_buf[...]
            g_buf[...] = dot_nt(x, x).astype(BF16)
            g = g_buf[...]
            mixed = (-4.775 * g.astype(F32) + 2.0315 * dot(g, g)).astype(BF16)
            x_buf[...] = 3.4445 * x.astype(F32) + dot(mixed, x)
            m_buf[...] = x_buf[...].astype(BF16)
        edges = (
            (0, z < Z - 1, {"tok": me + 4}), (1, z > 0, {"tok": me - 4}),
            (3, True, across), (2, True, sibling),
        )
        for i in range(CHUNKS):
            rows = slice(i * R, (i + 1) * R)
            old = w_ref[owned_w, rows, :].astype(F32)
            fresh = old - m_buf[rows, :].astype(F32)
            scale = jnp.sqrt(
                (jnp.mean(old * old, axis=1, keepdims=True) + 1e-06)
                / (jnp.mean(fresh * fresh, axis=1, keepdims=True) + 1e-06)
            )
            wn[y, owned_w, rows, :] = (fresh * scale).astype(BF16)
            w_copies(y, owned_w, i, edges)

    def spread_all(ws):
        routes = []
        end = 0
        for home in (True, False):
            h = y if home else 1 - y
            for w in ws:
                hops = jnp.abs(z - owner_z(w, h)) + (0 if home else 1)
                start = LAG * (hops - 1) + (0 if home else LEAF)
                routes.append((h, w, start, hops > 0, w_targets(w, home)))
                end = jnp.maximum(end, start + CHUNKS)

        def step(t, _):
            for h, w, start, live, targets in routes:
                i = t - start

                @pl.when(jnp.logical_and(live, jnp.logical_and(i >= 0, i < CHUNKS)))
                def _():
                    wait_block(h, w, i)
                    w_copies(h, w, i, targets)

            return 0

        lax.fori_loop(0, end, step, 0)

    @pl.when(pair)
    def _():
        spread_all((0, 1))

    @pl.when(jnp.logical_not(pair))
    def _():
        spread_all((2,))

    def save(h, w):
        return pltpu.make_async_copy(wn.at[h, w], neww_ref.at[h, w], out_sem.at[0])

    for mine_first in (True, False):
        for w in range(3):

            @pl.when((pair == (w < 2)) == mine_first)
            def _():
                for h in range(HEADS):
                    if not mine_first:
                        w_wait(h, w, 2).wait_recv()
                    save(h, w).start()

    loads[4].wait()

    for kind in range(2):
        token_wait(kind).wait_send()

    @pl.when(pair)
    def _():
        token_wait(2).wait_send()

    for w in range(3):
        moved = jnp.logical_and(pair == (w < 2), z != owner_z(w, y))

        @pl.when(jnp.logical_and(moved, jnp.logical_not(starts(w))) if w < 2 else moved)
        def _():
            chain_sent(w, 0).wait_send()

        @pl.when(moved)
        def _():
            chain_sent(w, 1).wait_send()

        @pl.when(pair == (w < 2))
        def _():
            for home in (True, False):
                h = y if home else 1 - y
                for kind, go, _ in w_targets(w, home):

                    @pl.when(go)
                    def _():
                        w_wait(h, w, kind).wait_send()

    pltpu.make_async_copy(wn, neww_ref, out_sem.at[0]).wait()


def readout(query_ref, w_ref, out, w_out, out_v, sem):
    copies = [
        pltpu.make_async_copy(w_ref, w_out, sem.at[0]),
        pltpu.make_async_copy(out_v, out, sem.at[1]),
    ]
    copies[0].start()
    D = w_ref.shape[2]
    for h in range(HEADS):
        cols = slice(h * D, (h + 1) * D)
        query = query_ref[:, cols]
        gate = dot(query, w_ref[h, 0])
        upper = dot(query, w_ref[h, 1])
        hidden = (gate * jax.nn.sigmoid(gate) * upper).astype(BF16)
        out_v[:, cols] = dot(hidden, w_ref[h, 2]).astype(BF16)
    copies[1].start()
    for cp in copies:
        cp.wait()


def body(Z, keys, values, queries, rates, fast_weights):
    D = fast_weights.shape[2]
    tokens = keys.shape[0]
    rows = tokens * 4
    sums = D * D // (SUM_ROWS * SUM_COLS)
    vmem = pl.BlockSpec(memory_space=pltpu.VMEM)
    hbm = pl.BlockSpec(memory_space=pltpu.MemorySpace.HBM)

    def run(*refs):
        kernel(Z, *refs)

    query, fresh = pl.pallas_call(
        run,
        out_shape=(
            jax.ShapeDtypeStruct((tokens, HEADS * D), BF16),
            jax.ShapeDtypeStruct((HEADS, 3, D, D), BF16),
        ),
        in_specs=[hbm] * 5,
        out_specs=(pl.BlockSpec(memory_space=pl.ANY), pl.BlockSpec(memory_space=pl.ANY)),
        scratch_shapes=[
            pltpu.VMEM((tokens, HEADS * D), BF16),
            pltpu.VMEM(rates.shape, F32),
            pltpu.VMEM((3, D, D), BF16),
            pltpu.VMEM((HEADS, tokens, D), BF16),
            pltpu.VMEM((rows, D), BF16),
            pltpu.VMEM((rows, D), BF16),
            pltpu.VMEM((2, rows, D), F32),
            pltpu.VMEM((2, rows, D), BF16),
            pltpu.VMEM((2, sums, SUM_ROWS, SUM_COLS), BF16),
            pltpu.VMEM((2, sums, SUM_ROWS, SUM_COLS), BF16),
            pltpu.VMEM((SUM_ROWS, SUM_COLS), F32),
            pltpu.VMEM((D, D), BF16),
            pltpu.VMEM((D, D), F32),
            pltpu.VMEM((D, D), BF16),
            pltpu.VMEM((HEADS, 3, D, D), BF16),
            pltpu.SemaphoreType.DMA((3,)),
            pltpu.SemaphoreType.DMA((2, 4)),
            pltpu.SemaphoreType.DMA((2, 2)),
            pltpu.SemaphoreType.DMA((2, sums)),
            pltpu.SemaphoreType.DMA((4, 4)),
            pltpu.SemaphoreType.DMA((4, CHUNKS)),
            pltpu.SemaphoreType.DMA((4,)),
            pltpu.SemaphoreType.DMA((1,)),
            pltpu.SemaphoreType.DMA((5,)),
            pltpu.SemaphoreType.REGULAR,
        ],
        compiler_params=pltpu.CompilerParams(
            collective_id=0, has_side_effects=True, vmem_limit_bytes=30 * 1024 * 1024
        ),
        name="ttt_step",
    )(*[pltpu.with_memory_space_constraint(a, pltpu.MemorySpace.HBM) for a in (keys, values, queries, rates, fast_weights)])
    return pl.pallas_call(
        readout,
        out_shape=(
            jax.ShapeDtypeStruct(query.shape, BF16),
            jax.ShapeDtypeStruct(fresh.shape, BF16),
        ),
        in_specs=[vmem] * 2,
        out_specs=(hbm, hbm),
        scratch_shapes=[
            pltpu.VMEM(query.shape, BF16),
            pltpu.SemaphoreType.DMA((2,)),
        ],
        compiler_params=pltpu.CompilerParams(vmem_limit_bytes=4 * 1024 * 1024),
        name="readout",
    )(query, fresh)


def solution(mesh):
    Z = mesh.shape["tok"] // 4
    return jax.shard_map(
        functools.partial(body, Z),
        mesh=mesh,
        in_specs=(
            P(("grp", "tok"), None),
            P(("grp", "tok"), None),
            P(("grp", "tok"), None),
            P(None, ("grp", "tok")),
            P(),
        ),
        out_specs=(P(("grp", "tok"), None), P("grp", None, None, None)),
        check_vma=False,
    )
```

```python
import functools

import jax
import jax.numpy as jnp
from jax import lax
from jax.experimental import pallas as pl
from jax.experimental.pallas import tpu as pltpu
from jax.sharding import PartitionSpec as P

HEADS = 2
NS_STEPS = 2
CHUNKS = 16
SUM_CHUNKS = 16
SUM_LAG = 7
LAG = 6
LEAF = 16
SHIFT = 0
MESH = pl.DeviceIdType.MESH
F32 = jnp.float32
BF16 = jnp.bfloat16


def dot(a, b):
    return jnp.dot(a, b, preferred_element_type=F32)


def dot_nt(a, b):
    return lax.dot_general(a, b, (((1,), (1,)), ((), ())), preferred_element_type=F32)


def dot_tn(a, b):
    return lax.dot_general(a, b, (((0,), (0,)), ((), ())), preferred_element_type=F32)


def kernel(
    Z,
    k_hbm, v_hbm, q_hbm, r_hbm, w_hbm,
    query_ref, neww_ref,
    v_ref, r_ref, w_ref,
    o_loc, keys, outer, gates, grads, sums, recv, sendbuf, square, m_buf, x_buf, g_buf, wn,
    tok_send, tok_recv, chain_send, chain_recv, w_send, w_recv, s_recv, out_sem, in_sem,
):
    tokens = k_hbm.shape[0]
    D = w_ref.shape[1]
    R = D // CHUNKS
    S = D // SUM_CHUNKS
    me = lax.axis_index("tok")
    c = me % 2
    y = (me // 2) % 2
    z = me // 4

    def mid(h):
        return Z // 2 - 1 + SHIFT * h

    def at(zz, yy, cc):
        return {"tok": (zz * 2 + yy) * 2 + cc}

    def block_rows(p):
        return pl.ds(pl.multiple_of(p * tokens, tokens), tokens)

    def head_cols(h):
        return pl.ds(pl.multiple_of(h * D, D), D)

    sibling = at(z, y, 1 - c)
    across = at(z, 1 - y, c)
    mine = y * 2 + c
    pair = c == 1
    gatherer = at(z, 1 - y, 1)
    middle = z == mid(y)
    sums_here = jnp.logical_or(pair, middle)

    barrier = pltpu.get_barrier_semaphore()
    for peer in (sibling, across, at(z, 1 - y, 1 - c)):
        pl.semaphore_signal(barrier, inc=1, device_id=peer, device_id_type=MESH)

    @pl.when(z > 0)
    def _():
        pl.semaphore_signal(barrier, inc=1, device_id={"tok": me - 4}, device_id_type=MESH)

    @pl.when(z < Z - 1)
    def _():
        pl.semaphore_signal(barrier, inc=1, device_id={"tok": me + 4}, device_id_type=MESH)

    loads = [
        pltpu.make_async_copy(src, dst, in_sem.at[n])
        for n, (src, dst) in enumerate((
            (r_hbm, r_ref), (v_hbm, v_ref),
            (k_hbm.at[:, head_cols(y)], keys.at[block_rows(mine), :]),
            (w_hbm.at[y], w_ref), (q_hbm, query_ref),
        ))
    ]
    for load in loads:
        load.start()
    square[...] = jnp.zeros_like(square)

    def token_copy(a, kind):
        h = y if kind == 0 else 1 - y
        src = o_loc.at[h] if a else k_hbm.at[:, head_cols(h)]
        return pltpu.make_async_remote_copy(
            src, (keys, outer)[a].at[block_rows(mine), :],
            tok_send.at[kind], tok_recv.at[a, mine],
            device_id=gatherer if kind else sibling, device_id_type=MESH)

    def pass_on(a, p):
        block = (keys, outer)[a].at[block_rows(p), :]
        return pltpu.make_async_remote_copy(
            block, block, tok_send.at[2], tok_recv.at[a, p],
            device_id=sibling, device_id_type=MESH)

    def token_wait(kind):
        block = keys.at[pl.ds(0, tokens * (4 if kind == 2 else 2)), :]
        return pltpu.make_async_remote_copy(
            block, block, tok_send.at[kind], tok_recv.at[0, 0],
            device_id=sibling, device_id_type=MESH)

    def send_tokens(a):
        token_copy(a, 1).start()

        @pl.when(jnp.logical_or(jnp.logical_not(pair), middle))
        def _():
            token_copy(a, 0).start()

    pl.semaphore_wait(barrier, 3 + jnp.where(z > 0, 1, 0) + jnp.where(z < Z - 1, 1, 0))
    send_tokens(0)
    loads[0].wait()
    loads[1].wait()
    for h in range(HEADS):
        row = jnp.broadcast_to(r_ref[h : h + 1, :], (128, tokens))
        col = jnp.concatenate([row.T] * (D // 128), axis=1)
        o_loc[h] = (-col * v_ref[:, h * D : (h + 1) * D].astype(F32)).astype(BF16)

    send_tokens(1)
    outer[block_rows(mine), :] = o_loc[y]
    loads[2].wait()
    loads[3].wait()

    def forward_step(s, _):
        d = s // 4 * 2 + s % 2
        p = jnp.where(d < 2, y * 2 + jnp.where(d == 0, c, 1 - c), (1 - y) * 2 + d % 2)
        rows = block_rows(p)
        for a in range(2):

            @pl.when(jnp.logical_and(s // 2 % 2 == a, d > 0))
            def _():
                pass_on(a, p).wait_recv()

                @pl.when(jnp.logical_and(jnp.logical_and(pair, middle), d >= 2))
                def _():
                    pass_on(a, p).start()

        @pl.when(s // 2 % 2 == 0)
        def _():
            key = keys[rows, :]
            gate = dot(key, w_ref[0])
            upper = dot(key, w_ref[1])

            gates[0, rows, :] = gate
            gates[1, rows, :] = upper
            grads[2, rows, :] = (gate * jax.nn.sigmoid(gate) * upper).astype(BF16)

        @pl.when(jnp.logical_and(pair, s // 2 % 2 == 1))
        def _():
            gate = gates[0, rows, :]
            upper = gates[1, rows, :]
            back = dot_nt(outer[rows, :], w_ref[2])
            sigma = jax.nn.sigmoid(gate)
            grads[0, rows, :] = (back * upper * sigma * (1.0 + gate * (1.0 - sigma))).astype(BF16)
            grads[1, rows, :] = (back * (gate * sigma)).astype(BF16)

        return 0

    lax.fori_loop(0, jnp.where(sums_here, 8, 0), forward_step, 0)

    def owner_z(w, h):
        return (0, Z - 1, mid(h))[w]

    def chain_copy(w, i, step, side):
        there = z + step == mid(y)
        held = jnp.where(there, side, 2) if w == 2 else w
        core = jnp.where(there, 0, 1) if w == 2 else 1
        return pltpu.make_async_remote_copy(
            sendbuf.at[w, i], recv.at[held, i], chain_send.at[w], chain_recv.at[held, i],
            device_id=at(z + step, y, core), device_id_type=MESH)

    def chain_sent(w):
        block = sendbuf.at[w]
        return pltpu.make_async_remote_copy(
            block, block, chain_send.at[w], chain_recv.at[w, 0],
            device_id=sibling, device_id_type=MESH)

    def chain_roles(w):
        own = owner_z(w, y)
        return (
            jnp.logical_and(z > 0, z <= own), jnp.logical_and(z < Z - 1, z >= own),
            z == own, z < own, z > own,
        )

    def reduce_event(w, i, roles):
        below, above, ends, rises, falls = roles
        rows = pl.ds(pl.multiple_of(i * S, S), S)

        def take(side):
            held = jnp.where(middle, side, 2) if w == 2 else w
            block = recv.at[held, i]
            pltpu.make_async_remote_copy(
                block, block, chain_send.at[w], chain_recv.at[held, i],
                device_id=sibling, device_id_type=MESH).wait_recv()
            sums[w, rows, :] += recv[held, i].astype(F32)

        @pl.when(below)
        def _():
            take(0)

        @pl.when(above)
        def _():
            take(1)

        @pl.when(ends)
        def _():
            rounded = sums[w, rows, :].astype(BF16)
            m_buf[rows, :] = rounded
            square[...] += jnp.square(rounded.astype(F32))

        @pl.when(jnp.logical_not(ends))
        def _():
            sendbuf[w, i] = sums[w, rows, :].astype(BF16)

        @pl.when(rises)
        def _():
            chain_copy(w, i, 1, 0).start()

        @pl.when(falls)
        def _():
            chain_copy(w, i, -1, 1).start()

    def depth(w):
        own = owner_z(w, y)
        rise = jnp.where(z <= own, z, 0)
        fall = jnp.where(z >= own, Z - 1 - z, 0)
        return SUM_LAG * jnp.maximum(rise, fall)

    def reduce_all(ws, depths, live):
        roles = [chain_roles(w) for w in ws]

        def step(t, _):
            for w, lag, role, on in zip(ws, depths, roles, live):
                i = t - lag

                @pl.when(jnp.logical_and(on, jnp.logical_and(i >= 0, i < SUM_CHUNKS)))
                def _():
                    reduce_event(w, i, role)

            return 0

        return step

    @pl.when(pair)
    def _():
        depths = [depth(0), depth(1), depth(2) + SUM_CHUNKS]
        step = reduce_all((0, 1, 2), depths, (True, True, jnp.logical_not(middle)))
        near = jnp.where(2 * z < Z, 1, 0)
        edge = jnp.logical_or(z == 0, z == Z - 1)
        first = jnp.where(edge, SUM_CHUNKS, 0)

        def near_part(n, _):
            rows = pl.ds(pl.multiple_of(n * (D // 4), D // 4), D // 4)
            sums[near, rows, :] = dot_tn(keys[:, rows], grads[near])
            lax.fori_loop(first * n // 4, first * (n + 1) // 4, step, 0)
            return 0

        lax.fori_loop(0, 4, near_part, 0)
        sums[1 - near] = dot_tn(keys[...], grads[1 - near])
        sums[2] = dot_tn(grads[2], outer[...])
        lax.fori_loop(first, SUM_CHUNKS + functools.reduce(jnp.maximum, depths), step, 0)

    @pl.when(jnp.logical_and(jnp.logical_not(pair), middle))
    def _():
        sums[2] = dot_tn(grads[2], outer[...])
        lax.fori_loop(0, SUM_CHUNKS, reduce_all((2,), (0,), (True,)), 0)

    def owns(w):
        return jnp.logical_and(pair == (w < 2), z == owner_z(w, y))

    def stream(h, w):
        return h * 2 + w % 2

    def w_targets(w, home):
        own = owner_z(w, y)
        leaf = (2, True, sibling)
        if not home:
            return (leaf,)
        return (
            (0, jnp.logical_and(z >= own, z < Z - 1), {"tok": me + 4}),
            (1, jnp.logical_and(z <= own, z > 0), {"tok": me - 4}),
            (3, True, across),
            leaf,
        )

    def arrival(w, leaf, i):
        return w_recv.at[w % 2, i] if leaf else chain_recv.at[w % 2, i]

    def w_copies(h, w, i, targets):
        rows = pl.ds(pl.multiple_of(i * R, R), R)
        block = wn.at[h, w, rows, :]
        n = stream(h, w)

        def copy(kind, dev):
            pltpu.make_async_remote_copy(
                block, block, w_send.at[n, kind], arrival(w, kind == 3, i) if kind != 2 else s_recv.at[n],
                device_id=dev, device_id_type=MESH).start()

        for kind, go, dev in targets:
            if go is True:
                copy(kind, dev)
            else:

                @pl.when(go)
                def _():
                    copy(kind, dev)

    def w_wait(h, w, kind):
        block = wn.at[h, w]
        n = stream(h, w)
        return pltpu.make_async_remote_copy(
            block, block, w_send.at[n, kind], s_recv.at[n],
            device_id=sibling, device_id_type=MESH)

    def wait_block(h, w, i, leaf):
        rows = pl.ds(pl.multiple_of(i * R, R), R)
        block = wn.at[h, w, rows, :]
        n = stream(h, w)
        pltpu.make_async_remote_copy(
            block, block, w_send.at[n, 2], arrival(w, leaf, i),
            device_id=sibling, device_id_type=MESH).wait_recv()

    is_owner = functools.reduce(jnp.logical_or, [owns(w) for w in range(3)])
    owned_w = jnp.where(owns(0), 0, jnp.where(owns(1), 1, 2))

    @pl.when(is_owner)
    def _():
        norm = jnp.sqrt(jnp.sum(square[...])) + 1e-07
        m_buf[...] = (m_buf[...].astype(F32) / norm).astype(BF16)
        for step in range(NS_STEPS):
            x = m_buf[...]
            g_buf[...] = dot_nt(x, x).astype(BF16)
            g = g_buf[...]
            mixed = (-4.775 * g.astype(F32) + 2.0315 * dot(g, g)).astype(BF16)
            x_buf[...] = 3.4445 * x.astype(F32) + dot(mixed, x)
            m_buf[...] = x_buf[...].astype(BF16)
        edges = (
            (0, z < Z - 1, {"tok": me + 4}), (1, z > 0, {"tok": me - 4}),
            (3, True, across), (2, True, sibling),
        )
        for i in range(CHUNKS):
            rows = slice(i * R, (i + 1) * R)
            old = w_ref[owned_w, rows, :].astype(F32)
            fresh = old - m_buf[rows, :].astype(F32)
            scale = jnp.sqrt(
                (jnp.mean(old * old, axis=1, keepdims=True) + 1e-06)
                / (jnp.mean(fresh * fresh, axis=1, keepdims=True) + 1e-06)
            )
            wn[y, owned_w, rows, :] = (fresh * scale).astype(BF16)
            w_copies(y, owned_w, i, edges)

    def spread_all(ws):
        routes = []
        end = 0
        for home in (True, False):
            h = y if home else 1 - y
            for w in ws:
                hops = jnp.abs(z - owner_z(w, h)) + (0 if home else 1)
                start = LAG * (hops - 1) + (0 if home else LEAF)
                routes.append((h, w, start, hops > 0, w_targets(w, home)))
                end = jnp.maximum(end, start + CHUNKS)

        def step(t, _):
            for h, w, start, live, targets in routes:
                i = t - start

                @pl.when(jnp.logical_and(live, jnp.logical_and(i >= 0, i < CHUNKS)))
                def _():
                    wait_block(h, w, i, len(targets) == 1)
                    w_copies(h, w, i, targets)

            return 0

        lax.fori_loop(0, end, step, 0)

    @pl.when(pair)
    def _():
        spread_all((0, 1))

    @pl.when(jnp.logical_not(pair))
    def _():
        spread_all((2,))

    def save(h, w):
        return pltpu.make_async_copy(wn.at[h, w], neww_ref.at[h, w], out_sem.at[0])

    for mine_first in (True, False):
        for w in range(3):

            @pl.when((pair == (w < 2)) == mine_first)
            def _():
                for h in range(HEADS):
                    if not mine_first:
                        w_wait(h, w, 2).wait_recv()
                    save(h, w).start()

    loads[4].wait()

    token_wait(1).wait_send()

    @pl.when(jnp.logical_or(jnp.logical_not(pair), middle))
    def _():
        token_wait(0).wait_send()

    @pl.when(jnp.logical_and(pair, middle))
    def _():
        token_wait(2).wait_send()

    for w in range(3):

        @pl.when(jnp.logical_and(pair, z != owner_z(w, y)))
        def _():
            chain_sent(w).wait_send()

        @pl.when(pair == (w < 2))
        def _():
            for home in (True, False):
                h = y if home else 1 - y
                for kind, go, _ in w_targets(w, home):

                    @pl.when(go)
                    def _():
                        w_wait(h, w, kind).wait_send()

    pltpu.make_async_copy(wn, neww_ref, out_sem.at[0]).wait()


def readout(query_ref, w_ref, out, w_out, out_v, sem):
    copies = [
        pltpu.make_async_copy(w_ref, w_out, sem.at[0]),
        pltpu.make_async_copy(out_v, out, sem.at[1]),
    ]
    copies[0].start()
    D = w_ref.shape[2]
    for h in range(HEADS):
        cols = slice(h * D, (h + 1) * D)
        query = query_ref[:, cols]
        gate = dot(query, w_ref[h, 0])
        upper = dot(query, w_ref[h, 1])
        hidden = (gate * jax.nn.sigmoid(gate) * upper).astype(BF16)
        out_v[:, cols] = dot(hidden, w_ref[h, 2]).astype(BF16)
    copies[1].start()
    for cp in copies:
        cp.wait()


def body(Z, keys, values, queries, rates, fast_weights):
    D = fast_weights.shape[2]
    tokens = keys.shape[0]
    rows = tokens * 4
    vmem = pl.BlockSpec(memory_space=pltpu.VMEM)
    hbm = pl.BlockSpec(memory_space=pltpu.MemorySpace.HBM)

    def run(*refs):
        kernel(Z, *refs)

    query, fresh = pl.pallas_call(
        run,
        out_shape=(
            jax.ShapeDtypeStruct((tokens, HEADS * D), BF16),
            jax.ShapeDtypeStruct((HEADS, 3, D, D), BF16),
        ),
        in_specs=[hbm] * 5,
        out_specs=(pl.BlockSpec(memory_space=pl.ANY), pl.BlockSpec(memory_space=pl.ANY)),
        scratch_shapes=[
            pltpu.VMEM((tokens, HEADS * D), BF16),
            pltpu.VMEM(rates.shape, F32),
            pltpu.VMEM((3, D, D), BF16),
            pltpu.VMEM((HEADS, tokens, D), BF16),
            pltpu.VMEM((rows, D), BF16),
            pltpu.VMEM((rows, D), BF16),
            pltpu.VMEM((2, rows, D), F32),
            pltpu.VMEM((3, rows, D), BF16),
            pltpu.VMEM((3, D, D), F32),
            pltpu.VMEM((3, SUM_CHUNKS, D // SUM_CHUNKS, D), BF16),
            pltpu.VMEM((3, SUM_CHUNKS, D // SUM_CHUNKS, D), BF16),
            pltpu.VMEM((D // SUM_CHUNKS, D), F32),
            pltpu.VMEM((D, D), BF16),
            pltpu.VMEM((D, D), F32),
            pltpu.VMEM((D, D), BF16),
            pltpu.VMEM((HEADS, 3, D, D), BF16),
            pltpu.SemaphoreType.DMA((3,)),
            pltpu.SemaphoreType.DMA((2, 4)),
            pltpu.SemaphoreType.DMA((3,)),
            pltpu.SemaphoreType.DMA((3, SUM_CHUNKS)),
            pltpu.SemaphoreType.DMA((4, 4)),
            pltpu.SemaphoreType.DMA((2, CHUNKS)),
            pltpu.SemaphoreType.DMA((4,)),
            pltpu.SemaphoreType.DMA((1,)),
            pltpu.SemaphoreType.DMA((5,)),
        ],
        compiler_params=pltpu.CompilerParams(
            collective_id=0, has_side_effects=True, vmem_limit_bytes=30 * 1024 * 1024
        ),
        name="ttt_step",
    )(*[pltpu.with_memory_space_constraint(a, pltpu.MemorySpace.HBM) for a in (keys, values, queries, rates, fast_weights)])
    return pl.pallas_call(
        readout,
        out_shape=(
            jax.ShapeDtypeStruct(query.shape, BF16),
            jax.ShapeDtypeStruct(fresh.shape, BF16),
        ),
        in_specs=[vmem] * 2,
        out_specs=(hbm, hbm),
        scratch_shapes=[
            pltpu.VMEM(query.shape, BF16),
            pltpu.SemaphoreType.DMA((2,)),
        ],
        compiler_params=pltpu.CompilerParams(vmem_limit_bytes=4 * 1024 * 1024),
        name="readout",
    )(query, fresh)


def solution(mesh):
    Z = mesh.shape["tok"] // 4
    return jax.shard_map(
        functools.partial(body, Z),
        mesh=mesh,
        in_specs=(
            P(("grp", "tok"), None),
            P(("grp", "tok"), None),
            P(("grp", "tok"), None),
            P(None, ("grp", "tok")),
            P(),
        ),
        out_specs=(P(("grp", "tok"), None), P("grp", None, None, None)),
        check_vma=False,
    )
```

```python
import functools

import jax
import jax.numpy as jnp
from jax import lax
from jax.experimental import pallas as pl
from jax.experimental.pallas import tpu as pltpu
from jax.sharding import PartitionSpec as P

HEADS = 2
NS_BLOCKS = 4
CHUNKS = 16
SUM_CHUNKS = 16
SUM_LAG = 7
LAG = 6
LEAF = 16
LEAF_END = 8
LATE = 6
SHIFT = 0
MESH = pl.DeviceIdType.MESH
F32 = jnp.float32
BF16 = jnp.bfloat16


def dot(a, b):
    return jnp.dot(a, b, preferred_element_type=F32)


def dot_nt(a, b):
    return lax.dot_general(a, b, (((1,), (1,)), ((), ())), preferred_element_type=F32)


def dot_tn(a, b):
    return lax.dot_general(a, b, (((0,), (0,)), ((), ())), preferred_element_type=F32)


def kernel(
    Z,
    k_hbm, v_hbm, q_hbm, r_hbm, w_hbm,
    query_ref, neww_ref,
    v_ref, r_ref, w_ref,
    o_loc, keys, outer, gates, grads, sums, recv, sendbuf, square, m_buf, x_buf, g_buf, mix_buf, wn,
    tok_send, tok_recv, chain_send, chain_recv, w_send, w_recv, s_recv, out_sem, in_sem,
):
    tokens = k_hbm.shape[0]
    D = w_ref.shape[1]
    R = D // CHUNKS
    S = D // SUM_CHUNKS
    me = lax.axis_index("tok")
    c = me % 2
    y = (me // 2) % 2
    z = me // 4

    def mid(h):
        return Z // 2 - 1 + SHIFT * h

    def at(zz, yy, cc):
        return {"tok": (zz * 2 + yy) * 2 + cc}

    def block_rows(p):
        return pl.ds(pl.multiple_of(p * tokens, tokens), tokens)

    def head_cols(h):
        return pl.ds(pl.multiple_of(h * D, D), D)

    sibling = at(z, y, 1 - c)
    across = at(z, 1 - y, c)
    mine = y * 2 + c
    pair = c == 1
    gatherer = at(z, 1 - y, 1)
    middle = z == mid(y)
    sums_here = jnp.logical_or(pair, middle)

    barrier = pltpu.get_barrier_semaphore()
    for peer in (sibling, across, at(z, 1 - y, 1 - c)):
        pl.semaphore_signal(barrier, inc=1, device_id=peer, device_id_type=MESH)

    @pl.when(z > 0)
    def _():
        pl.semaphore_signal(barrier, inc=1, device_id={"tok": me - 4}, device_id_type=MESH)

    @pl.when(z < Z - 1)
    def _():
        pl.semaphore_signal(barrier, inc=1, device_id={"tok": me + 4}, device_id_type=MESH)

    loads = [
        pltpu.make_async_copy(src, dst, in_sem.at[n])
        for n, (src, dst) in enumerate((
            (r_hbm, r_ref), (v_hbm, v_ref),
            (k_hbm.at[:, head_cols(y)], keys.at[block_rows(mine), :]),
            (w_hbm.at[y], w_ref), (q_hbm, query_ref),
        ))
    ]
    for load in loads:
        load.start()
    square[...] = jnp.zeros_like(square)

    def token_copy(a, kind):
        h = y if kind == 0 else 1 - y
        src = o_loc.at[h] if a else k_hbm.at[:, head_cols(h)]
        return pltpu.make_async_remote_copy(
            src, (keys, outer)[a].at[block_rows(mine), :],
            tok_send.at[kind], tok_recv.at[a, mine],
            device_id=gatherer if kind else sibling, device_id_type=MESH)

    def pass_on(a, p):
        block = (keys, outer)[a].at[block_rows(p), :]
        return pltpu.make_async_remote_copy(
            block, block, tok_send.at[2], tok_recv.at[a, p],
            device_id=sibling, device_id_type=MESH)

    def token_wait(kind):
        block = keys.at[pl.ds(0, tokens * (4 if kind == 2 else 2)), :]
        return pltpu.make_async_remote_copy(
            block, block, tok_send.at[kind], tok_recv.at[0, 0],
            device_id=sibling, device_id_type=MESH)

    def send_tokens(a):
        token_copy(a, 1).start()

        @pl.when(jnp.logical_or(jnp.logical_not(pair), middle))
        def _():
            token_copy(a, 0).start()

    pl.semaphore_wait(barrier, 3 + jnp.where(z > 0, 1, 0) + jnp.where(z < Z - 1, 1, 0))
    send_tokens(0)
    loads[0].wait()
    loads[1].wait()
    for h in range(HEADS):
        row = jnp.broadcast_to(r_ref[h : h + 1, :], (128, tokens))
        col = jnp.concatenate([row.T] * (D // 128), axis=1)
        o_loc[h] = (-col * v_ref[:, h * D : (h + 1) * D].astype(F32)).astype(BF16)

    send_tokens(1)
    outer[block_rows(mine), :] = o_loc[y]
    loads[2].wait()
    loads[3].wait()

    def forward_step(s, _):
        d = s // 4 * 2 + s % 2
        p = jnp.where(d < 2, y * 2 + jnp.where(d == 0, c, 1 - c), (1 - y) * 2 + d % 2)
        rows = block_rows(p)
        for a in range(2):

            @pl.when(jnp.logical_and(s // 2 % 2 == a, d > 0))
            def _():
                pass_on(a, p).wait_recv()

                @pl.when(jnp.logical_and(jnp.logical_and(pair, middle), d >= 2))
                def _():
                    pass_on(a, p).start()

        @pl.when(s // 2 % 2 == 0)
        def _():
            key = keys[rows, :]
            gate = dot(key, w_ref[0])
            upper = dot(key, w_ref[1])

            gates[0, rows, :] = gate
            gates[1, rows, :] = upper
            grads[2, rows, :] = (gate * jax.nn.sigmoid(gate) * upper).astype(BF16)

        @pl.when(jnp.logical_and(pair, s // 2 % 2 == 1))
        def _():
            gate = gates[0, rows, :]
            upper = gates[1, rows, :]
            back = dot_nt(outer[rows, :], w_ref[2])
            sigma = jax.nn.sigmoid(gate)
            grads[0, rows, :] = (back * upper * sigma * (1.0 + gate * (1.0 - sigma))).astype(BF16)
            grads[1, rows, :] = (back * (gate * sigma)).astype(BF16)

        return 0

    lax.fori_loop(0, jnp.where(sums_here, 8, 0), forward_step, 0)

    def owner_z(w, h):
        return (0, Z - 1, mid(h))[w]

    def chain_copy(w, i, step, side):
        there = z + step == mid(y)
        held = jnp.where(there, side, 2) if w == 2 else w
        core = jnp.where(there, 0, 1) if w == 2 else 1
        return pltpu.make_async_remote_copy(
            sendbuf.at[w, i], recv.at[held, i], chain_send.at[w], chain_recv.at[held, i],
            device_id=at(z + step, y, core), device_id_type=MESH)

    def chain_sent(w):
        block = sendbuf.at[w]
        return pltpu.make_async_remote_copy(
            block, block, chain_send.at[w], chain_recv.at[w, 0],
            device_id=sibling, device_id_type=MESH)

    def chain_roles(w):
        own = owner_z(w, y)
        return (
            jnp.logical_and(z > 0, z <= own), jnp.logical_and(z < Z - 1, z >= own),
            z == own, z < own, z > own,
        )

    def reduce_event(w, i, roles):
        below, above, ends, rises, falls = roles
        rows = pl.ds(pl.multiple_of(i * S, S), S)

        def take(side):
            held = jnp.where(middle, side, 2) if w == 2 else w
            block = recv.at[held, i]
            pltpu.make_async_remote_copy(
                block, block, chain_send.at[w], chain_recv.at[held, i],
                device_id=sibling, device_id_type=MESH).wait_recv()
            sums[w, rows, :] += recv[held, i].astype(F32)

        @pl.when(below)
        def _():
            take(0)

        @pl.when(above)
        def _():
            take(1)

        @pl.when(ends)
        def _():
            rounded = sums[w, rows, :].astype(BF16)
            m_buf[rows, :] = rounded
            square[...] += jnp.square(rounded.astype(F32))

        @pl.when(jnp.logical_not(ends))
        def _():
            sendbuf[w, i] = sums[w, rows, :].astype(BF16)

        @pl.when(rises)
        def _():
            chain_copy(w, i, 1, 0).start()

        @pl.when(falls)
        def _():
            chain_copy(w, i, -1, 1).start()

    def depth(w):
        own = owner_z(w, y)
        rise = jnp.where(z <= own, z, 0)
        fall = jnp.where(z >= own, Z - 1 - z, 0)
        return SUM_LAG * jnp.maximum(rise, fall)

    def reduce_all(ws, depths, live):
        roles = [chain_roles(w) for w in ws]

        def step(t, _):
            for w, lag, role, on in zip(ws, depths, roles, live):
                i = t - lag

                @pl.when(jnp.logical_and(on, jnp.logical_and(i >= 0, i < SUM_CHUNKS)))
                def _():
                    reduce_event(w, i, role)

            return 0

        return step

    @pl.when(pair)
    def _():
        depths = [depth(0), depth(1), depth(2) + SUM_CHUNKS]
        step = reduce_all((0, 1, 2), depths, (True, True, jnp.logical_not(middle)))
        near = jnp.where(2 * z < Z, 1, 0)
        edge = jnp.logical_or(z == 0, z == Z - 1)
        first = jnp.where(edge, SUM_CHUNKS, 0)

        def near_part(n, _):
            rows = pl.ds(pl.multiple_of(n * (D // 4), D // 4), D // 4)
            sums[near, rows, :] = dot_tn(keys[:, rows], grads[near])
            lax.fori_loop(first * n // 4, first * (n + 1) // 4, step, 0)
            return 0

        lax.fori_loop(0, 4, near_part, 0)
        sums[1 - near] = dot_tn(keys[...], grads[1 - near])
        sums[2] = dot_tn(grads[2], outer[...])
        lax.fori_loop(first, SUM_CHUNKS + functools.reduce(jnp.maximum, depths), step, 0)

    @pl.when(jnp.logical_and(jnp.logical_not(pair), middle))
    def _():
        sums[2] = dot_tn(grads[2], outer[...])
        lax.fori_loop(0, SUM_CHUNKS, reduce_all((2,), (0,), (True,)), 0)

    def owns(w):
        return jnp.logical_and(pair == (w < 2), z == owner_z(w, y))

    def stream(h, w):
        return h * 2 + w % 2

    def w_targets(w, home):
        own = owner_z(w, y)
        leaf = (2, True, sibling)
        if not home:
            return (leaf,)
        return (
            (0, jnp.logical_and(z >= own, z < Z - 1), {"tok": me + 4}),
            (1, jnp.logical_and(z <= own, z > (1 if w == 1 else 0)), {"tok": me - 4}),
            (3, True, across),
            leaf,
        )

    def arrival(w, leaf, i):
        return w_recv.at[w % 2, i] if leaf else chain_recv.at[w % 2, i]

    def w_copies(h, w, i, targets):
        rows = pl.ds(pl.multiple_of(i * R, R), R)
        block = wn.at[h, w, rows, :]
        n = stream(h, w)

        def copy(kind, dev):
            pltpu.make_async_remote_copy(
                block, block, w_send.at[n, kind], arrival(w, kind == 3, i) if kind != 2 else s_recv.at[n],
                device_id=dev, device_id_type=MESH).start()

        for kind, go, dev in targets:
            if go is True:
                copy(kind, dev)
            else:

                @pl.when(go)
                def _():
                    copy(kind, dev)

    def w_wait(h, w, kind):
        block = wn.at[h, w]
        n = stream(h, w)
        return pltpu.make_async_remote_copy(
            block, block, w_send.at[n, kind], s_recv.at[n],
            device_id=sibling, device_id_type=MESH)

    def wait_block(h, w, i, leaf):
        rows = pl.ds(pl.multiple_of(i * R, R), R)
        block = wn.at[h, w, rows, :]
        n = stream(h, w)
        pltpu.make_async_remote_copy(
            block, block, w_send.at[n, 2], arrival(w, leaf, i),
            device_id=sibling, device_id_type=MESH).wait_recv()

    is_owner = functools.reduce(jnp.logical_or, [owns(w) for w in range(3)])
    owned_w = jnp.where(owns(0), 0, jnp.where(owns(1), 1, 2))

    def renew(i, targets):
        rows = slice(i * R, (i + 1) * R)
        old = w_ref[owned_w, rows, :].astype(F32)
        fresh = old - m_buf[rows, :].astype(F32)
        scale = jnp.sqrt(
            (jnp.mean(old * old, axis=1, keepdims=True) + 1e-06)
            / (jnp.mean(fresh * fresh, axis=1, keepdims=True) + 1e-06)
        )
        wn[y, owned_w, rows, :] = (fresh * scale).astype(BF16)
        w_copies(y, owned_w, i, targets)

    @pl.when(is_owner)
    def _():
        scale = 1.0 / (jnp.sqrt(jnp.sum(square[...])) + 1e-07)

        def mix(x_ref, factor):
            x = x_ref[...]
            g_buf[...] = (dot_nt(x, x) * factor).astype(BF16)
            g = g_buf[...]
            mix_buf[...] = (-4.775 * g.astype(F32) + 2.0315 * dot(g, g)).astype(BF16)

        mix(m_buf, scale * scale)
        m = m_buf[...]
        x_buf[...] = ((3.4445 * m.astype(F32) + dot(mix_buf[...], m)) * scale).astype(BF16)
        mix(x_buf, 1.0)
        edges = (
            (0, z < Z - 1, {"tok": me + 4}), (1, z > 0, {"tok": me - 4}),
            (3, True, across), (2, True, sibling),
        )
        step_rows = D // NS_BLOCKS
        for b in range(NS_BLOCKS):
            wide = slice(b * step_rows, (b + 1) * step_rows)
            m_buf[wide, :] = (
                3.4445 * x_buf[wide, :].astype(F32) + dot(mix_buf[wide, :], x_buf[...])
            ).astype(BF16)
            for i in range(b * CHUNKS // NS_BLOCKS, (b + 1) * CHUNKS // NS_BLOCKS):
                renew(i, edges)

    def spread_all(ws):
        routes = []
        end = 0
        for home in (True, False):
            h = y if home else 1 - y
            for w in ws:
                away = jnp.abs(z - owner_z(w, h))
                hops = away + (0 if home else 1)
                edge = jnp.logical_or(z == 0, z == Z - 1)
                start = LAG * jnp.maximum(away - 1, 0)
                if not home:
                    start = start + jnp.where(away > 0, jnp.where(edge, LEAF_END, LEAF), 0)
                routes.append((h, w, start, hops > 0, True, w_targets(w, home), not home))
                end = jnp.maximum(end, start + CHUNKS)
                if home and w == 1:
                    down = [(1, True, {"tok": me - 4})]
                    routes.append((h, w, start + LATE, z == 1, False, down, False))
                    end = jnp.maximum(end, start + LATE + CHUNKS)

        def step(t, _):
            for h, w, start, live, waits, targets, leaf in routes:
                i = t - start

                @pl.when(jnp.logical_and(live, jnp.logical_and(i >= 0, i < CHUNKS)))
                def _():
                    if waits:
                        wait_block(h, w, i, leaf)
                    w_copies(h, w, i, targets)

            return 0

        lax.fori_loop(0, end, step, 0)

    @pl.when(pair)
    def _():
        spread_all((0, 1))

    @pl.when(jnp.logical_not(pair))
    def _():
        spread_all((2,))

    def save(h, w):
        return pltpu.make_async_copy(wn.at[h, w], neww_ref.at[h, w], out_sem.at[0])

    for mine_first in (True, False):
        for w in range(3):

            @pl.when((pair == (w < 2)) == mine_first)
            def _():
                for h in range(HEADS):
                    if not mine_first:
                        w_wait(h, w, 2).wait_recv()
                    save(h, w).start()

    loads[4].wait()

    token_wait(1).wait_send()

    @pl.when(jnp.logical_or(jnp.logical_not(pair), middle))
    def _():
        token_wait(0).wait_send()

    @pl.when(jnp.logical_and(pair, middle))
    def _():
        token_wait(2).wait_send()

    for w in range(3):

        @pl.when(jnp.logical_and(pair, z != owner_z(w, y)))
        def _():
            chain_sent(w).wait_send()

        @pl.when(pair == (w < 2))
        def _():
            for home in (True, False):
                h = y if home else 1 - y
                targets = w_targets(w, home)
                if home and w == 1:
                    targets += ((1, z == 1, None),)
                for kind, go, _ in targets:

                    @pl.when(go)
                    def _():
                        w_wait(h, w, kind).wait_send()

    pltpu.make_async_copy(wn, neww_ref, out_sem.at[0]).wait()


def readout(query_ref, w_ref, out, w_out, out_v, sem):
    copies = [
        pltpu.make_async_copy(w_ref, w_out, sem.at[0]),
        pltpu.make_async_copy(out_v, out, sem.at[1]),
    ]
    copies[0].start()
    D = w_ref.shape[2]
    for h in range(HEADS):
        cols = slice(h * D, (h + 1) * D)
        query = query_ref[:, cols]
        gate = dot(query, w_ref[h, 0])
        upper = dot(query, w_ref[h, 1])
        hidden = (gate * jax.nn.sigmoid(gate) * upper).astype(BF16)
        out_v[:, cols] = dot(hidden, w_ref[h, 2]).astype(BF16)
    copies[1].start()
    for cp in copies:
        cp.wait()


def body(Z, keys, values, queries, rates, fast_weights):
    D = fast_weights.shape[2]
    tokens = keys.shape[0]
    rows = tokens * 4
    vmem = pl.BlockSpec(memory_space=pltpu.VMEM)
    hbm = pl.BlockSpec(memory_space=pltpu.MemorySpace.HBM)

    def run(*refs):
        kernel(Z, *refs)

    query, fresh = pl.pallas_call(
        run,
        out_shape=(
            jax.ShapeDtypeStruct((tokens, HEADS * D), BF16),
            jax.ShapeDtypeStruct((HEADS, 3, D, D), BF16),
        ),
        in_specs=[hbm] * 5,
        out_specs=(pl.BlockSpec(memory_space=pl.ANY), pl.BlockSpec(memory_space=pl.ANY)),
        scratch_shapes=[
            pltpu.VMEM((tokens, HEADS * D), BF16),
            pltpu.VMEM(rates.shape, F32),
            pltpu.VMEM((3, D, D), BF16),
            pltpu.VMEM((HEADS, tokens, D), BF16),
            pltpu.VMEM((rows, D), BF16),
            pltpu.VMEM((rows, D), BF16),
            pltpu.VMEM((2, rows, D), F32),
            pltpu.VMEM((3, rows, D), BF16),
            pltpu.VMEM((3, D, D), F32),
            pltpu.VMEM((3, SUM_CHUNKS, D // SUM_CHUNKS, D), BF16),
            pltpu.VMEM((3, SUM_CHUNKS, D // SUM_CHUNKS, D), BF16),
            pltpu.VMEM((D // SUM_CHUNKS, D), F32),
            pltpu.VMEM((D, D), BF16),
            pltpu.VMEM((D, D), BF16),
            pltpu.VMEM((D, D), BF16),
            pltpu.VMEM((D, D), BF16),
            pltpu.VMEM((HEADS, 3, D, D), BF16),
            pltpu.SemaphoreType.DMA((3,)),
            pltpu.SemaphoreType.DMA((2, 4)),
            pltpu.SemaphoreType.DMA((3,)),
            pltpu.SemaphoreType.DMA((3, SUM_CHUNKS)),
            pltpu.SemaphoreType.DMA((4, 4)),
            pltpu.SemaphoreType.DMA((2, CHUNKS)),
            pltpu.SemaphoreType.DMA((4,)),
            pltpu.SemaphoreType.DMA((1,)),
            pltpu.SemaphoreType.DMA((5,)),
        ],
        compiler_params=pltpu.CompilerParams(
            collective_id=0, has_side_effects=True, vmem_limit_bytes=30 * 1024 * 1024
        ),
        name="ttt_step",
    )(*[pltpu.with_memory_space_constraint(a, pltpu.MemorySpace.HBM) for a in (keys, values, queries, rates, fast_weights)])
    return pl.pallas_call(
        readout,
        out_shape=(
            jax.ShapeDtypeStruct(query.shape, BF16),
            jax.ShapeDtypeStruct(fresh.shape, BF16),
        ),
        in_specs=[vmem] * 2,
        out_specs=(hbm, hbm),
        scratch_shapes=[
            pltpu.VMEM(query.shape, BF16),
            pltpu.SemaphoreType.DMA((2,)),
        ],
        compiler_params=pltpu.CompilerParams(vmem_limit_bytes=4 * 1024 * 1024),
        name="readout",
    )(query, fresh)


def solution(mesh):
    Z = mesh.shape["tok"] // 4
    return jax.shard_map(
        functools.partial(body, Z),
        mesh=mesh,
        in_specs=(
            P(("grp", "tok"), None),
            P(("grp", "tok"), None),
            P(("grp", "tok"), None),
            P(None, ("grp", "tok")),
            P(),
        ),
        out_specs=(P(("grp", "tok"), None), P("grp", None, None, None)),
        check_vma=False,
    )
```

```python
import functools

import jax
import jax.numpy as jnp
from jax import lax
from jax.experimental import pallas as pl
from jax.experimental.pallas import tpu as pltpu
from jax.sharding import PartitionSpec as P

HEADS = 2
NS_BLOCKS = 4
CHUNKS = 16
SUM_CHUNKS = 16
SUM_LAG = 7
LAG = 6
LEAF = 16
LEAF_END = 8
LATE = 6
SHIFT = 0
MESH = pl.DeviceIdType.MESH
F32 = jnp.float32
BF16 = jnp.bfloat16


def dot(a, b):
    return jnp.dot(a, b, preferred_element_type=F32)


def dot_nt(a, b):
    return lax.dot_general(a, b, (((1,), (1,)), ((), ())), preferred_element_type=F32)


def dot_tn(a, b):
    return lax.dot_general(a, b, (((0,), (0,)), ((), ())), preferred_element_type=F32)


def kernel(
    Z,
    k_hbm, v_hbm, q_hbm, r_hbm, w_hbm,
    query_ref, neww_ref,
    v_ref, r_ref, w_ref,
    o_loc, keys, outer, gates, grads, sums, recv, sendbuf, square, m_buf, x_buf, g_buf, mix_buf, wn,
    tok_send, tok_recv, chain_send, chain_recv, w_send, w_recv, s_recv, out_sem, in_sem,
):
    tokens = k_hbm.shape[0]
    D = w_ref.shape[1]
    R = D // CHUNKS
    S = D // SUM_CHUNKS
    me = lax.axis_index("tok")
    c = me % 2
    y = (me // 2) % 2
    z = me // 4

    def mid(h):
        return Z // 2 - 1 + SHIFT * h

    def at(zz, yy, cc):
        return {"tok": (zz * 2 + yy) * 2 + cc}

    def block_rows(p):
        return pl.ds(pl.multiple_of(p * tokens, tokens), tokens)

    def head_cols(h):
        return pl.ds(pl.multiple_of(h * D, D), D)

    sibling = at(z, y, 1 - c)
    across = at(z, 1 - y, c)
    mine = y * 2 + c
    pair = c == 1
    gatherer = at(z, 1 - y, 1)
    middle = z == mid(y)
    sums_here = jnp.logical_or(pair, middle)

    barrier = pltpu.get_barrier_semaphore()
    for peer in (sibling, across, at(z, 1 - y, 1 - c)):
        pl.semaphore_signal(barrier, inc=1, device_id=peer, device_id_type=MESH)

    @pl.when(z > 0)
    def _():
        pl.semaphore_signal(barrier, inc=1, device_id={"tok": me - 4}, device_id_type=MESH)

    @pl.when(z < Z - 1)
    def _():
        pl.semaphore_signal(barrier, inc=1, device_id={"tok": me + 4}, device_id_type=MESH)

    loads = [
        pltpu.make_async_copy(src, dst, in_sem.at[n])
        for n, (src, dst) in enumerate((
            (r_hbm, r_ref), (v_hbm, v_ref),
            (k_hbm.at[:, head_cols(y)], keys.at[block_rows(mine), :]),
            (w_hbm.at[y], w_ref), (q_hbm, query_ref),
        ))
    ]
    for load in loads:
        load.start()
    square[...] = jnp.zeros_like(square)

    def token_copy(a, kind):
        h = y if kind == 0 else 1 - y
        src = o_loc.at[h] if a else k_hbm.at[:, head_cols(h)]
        return pltpu.make_async_remote_copy(
            src, (keys, outer)[a].at[block_rows(mine), :],
            tok_send.at[kind], tok_recv.at[a, mine],
            device_id=gatherer if kind else sibling, device_id_type=MESH)

    def pass_on(a, p):
        block = (keys, outer)[a].at[block_rows(p), :]
        return pltpu.make_async_remote_copy(
            block, block, tok_send.at[2], tok_recv.at[a, p],
            device_id=sibling, device_id_type=MESH)

    def token_wait(kind):
        block = keys.at[pl.ds(0, tokens * (4 if kind == 2 else 2)), :]
        return pltpu.make_async_remote_copy(
            block, block, tok_send.at[kind], tok_recv.at[0, 0],
            device_id=sibling, device_id_type=MESH)

    def send_tokens(a):
        token_copy(a, 1).start()

        @pl.when(jnp.logical_or(jnp.logical_not(pair), middle))
        def _():
            token_copy(a, 0).start()

    pl.semaphore_wait(barrier, 3 + jnp.where(z > 0, 1, 0) + jnp.where(z < Z - 1, 1, 0))
    send_tokens(0)
    loads[0].wait()
    loads[1].wait()
    for h in range(HEADS):
        row = jnp.broadcast_to(r_ref[h : h + 1, :], (128, tokens))
        col = jnp.concatenate([row.T] * (D // 128), axis=1)
        o_loc[h] = (-col * v_ref[:, h * D : (h + 1) * D].astype(F32)).astype(BF16)

    send_tokens(1)
    outer[block_rows(mine), :] = o_loc[y]
    loads[2].wait()
    loads[3].wait()

    def forward_step(s, _):
        d = s // 4 * 2 + s % 2
        p = jnp.where(d < 2, y * 2 + jnp.where(d == 0, c, 1 - c), (1 - y) * 2 + d % 2)
        rows = block_rows(p)
        for a in range(2):

            @pl.when(jnp.logical_and(s // 2 % 2 == a, d > 0))
            def _():
                pass_on(a, p).wait_recv()

                @pl.when(jnp.logical_and(jnp.logical_and(pair, middle), d >= 2))
                def _():
                    pass_on(a, p).start()

        @pl.when(s // 2 % 2 == 0)
        def _():
            key = keys[rows, :]
            gate = dot(key, w_ref[0])
            upper = dot(key, w_ref[1])

            sigma = jax.nn.sigmoid(gate)
            silu_gate = gate * sigma
            gates[0, rows, :] = upper * sigma * (1.0 + gate * (1.0 - sigma))
            gates[1, rows, :] = silu_gate
            grads[2, rows, :] = (silu_gate * upper).astype(BF16)

        @pl.when(jnp.logical_and(pair, s // 2 % 2 == 1))
        def _():
            back = dot_nt(outer[rows, :], w_ref[2])
            grads[0, rows, :] = (back * gates[0, rows, :]).astype(BF16)
            grads[1, rows, :] = (back * gates[1, rows, :]).astype(BF16)

        return 0

    lax.fori_loop(0, jnp.where(sums_here, 8, 0), forward_step, 0)

    def owner_z(w, h):
        return (0, Z - 1, mid(h))[w]

    def chain_copy(w, i, step, side):
        there = z + step == mid(y)
        held = jnp.where(there, side, 2) if w == 2 else w
        core = jnp.where(there, 0, 1) if w == 2 else 1
        return pltpu.make_async_remote_copy(
            sendbuf.at[w, i], recv.at[held, i], chain_send.at[w], chain_recv.at[held, i],
            device_id=at(z + step, y, core), device_id_type=MESH)

    def chain_sent(w):
        block = sendbuf.at[w]
        return pltpu.make_async_remote_copy(
            block, block, chain_send.at[w], chain_recv.at[w, 0],
            device_id=sibling, device_id_type=MESH)

    def chain_roles(w):
        own = owner_z(w, y)
        return (
            jnp.logical_and(z > 0, z <= own), jnp.logical_and(z < Z - 1, z >= own),
            z == own, z < own, z > own,
        )

    def reduce_event(w, i, roles):
        below, above, ends, rises, falls = roles
        rows = pl.ds(pl.multiple_of(i * S, S), S)

        def take(side):
            held = jnp.where(middle, side, 2) if w == 2 else w
            block = recv.at[held, i]
            pltpu.make_async_remote_copy(
                block, block, chain_send.at[w], chain_recv.at[held, i],
                device_id=sibling, device_id_type=MESH).wait_recv()
            sums[w, rows, :] += recv[held, i].astype(F32)

        @pl.when(below)
        def _():
            take(0)

        @pl.when(above)
        def _():
            take(1)

        @pl.when(ends)
        def _():
            rounded = sums[w, rows, :].astype(BF16)
            m_buf[rows, :] = rounded
            square[...] += jnp.square(rounded.astype(F32))

        @pl.when(jnp.logical_not(ends))
        def _():
            sendbuf[w, i] = sums[w, rows, :].astype(BF16)

        @pl.when(rises)
        def _():
            chain_copy(w, i, 1, 0).start()

        @pl.when(falls)
        def _():
            chain_copy(w, i, -1, 1).start()

    def depth(w):
        own = owner_z(w, y)
        rise = jnp.where(z <= own, z, 0)
        fall = jnp.where(z >= own, Z - 1 - z, 0)
        return SUM_LAG * jnp.maximum(rise, fall)

    def reduce_all(ws, depths, live):
        roles = [chain_roles(w) for w in ws]

        def step(t, _):
            for w, lag, role, on in zip(ws, depths, roles, live):
                i = t - lag

                @pl.when(jnp.logical_and(on, jnp.logical_and(i >= 0, i < SUM_CHUNKS)))
                def _():
                    reduce_event(w, i, role)

            return 0

        return step

    @pl.when(pair)
    def _():
        depths = [depth(0), depth(1), depth(2) + SUM_CHUNKS]
        step = reduce_all((0, 1, 2), depths, (True, True, jnp.logical_not(middle)))
        near = jnp.where(2 * z < Z, 1, 0)
        edge = jnp.logical_or(z == 0, z == Z - 1)
        first = jnp.where(edge, SUM_CHUNKS, 0)

        def near_part(n, _):
            rows = pl.ds(pl.multiple_of(n * (D // 4), D // 4), D // 4)
            sums[near, rows, :] = dot_tn(keys[:, rows], grads[near])
            lax.fori_loop(first * n // 4, first * (n + 1) // 4, step, 0)
            return 0

        lax.fori_loop(0, 4, near_part, 0)
        sums[1 - near] = dot_tn(keys[...], grads[1 - near])
        sums[2] = dot_tn(grads[2], outer[...])
        lax.fori_loop(first, SUM_CHUNKS + functools.reduce(jnp.maximum, depths), step, 0)

    @pl.when(jnp.logical_and(jnp.logical_not(pair), middle))
    def _():
        sums[2] = dot_tn(grads[2], outer[...])
        lax.fori_loop(0, SUM_CHUNKS, reduce_all((2,), (0,), (True,)), 0)

    def owns(w):
        return jnp.logical_and(pair == (w < 2), z == owner_z(w, y))

    def w_targets(w, home):
        own = owner_z(w, y)
        leaf = (2, True, sibling)
        if not home:
            return (leaf,)
        return (
            (0, jnp.logical_and(z >= own, z < Z - 1), {"tok": me + 4}),
            (1, jnp.logical_and(z <= own, z > (1 if w == 1 else 0)), {"tok": me - 4}),
            (3, True, across),
            leaf,
        )

    def arrival(w, leaf, i):
        return w_recv.at[w % 2, i // 2] if leaf else chain_recv.at[w % 2, i]

    def w_copies(h, w, i, targets, size=1):
        rows = pl.ds(pl.multiple_of(i * R, R), size * R)
        block = wn.at[h, w, rows, :]

        def copy(kind, dev):
            pltpu.make_async_remote_copy(
                block, block, w_send.at[kind],
                arrival(w, kind == 3, i) if kind != 2 else s_recv.at[0],
                device_id=dev, device_id_type=MESH).start()

        for kind, go, dev in targets:
            if go is True:
                copy(kind, dev)
            else:

                @pl.when(go)
                def _():
                    copy(kind, dev)

    def w_wait(block, kind):
        return pltpu.make_async_remote_copy(
            block, block, w_send.at[kind], s_recv.at[0],
            device_id=sibling, device_id_type=MESH)

    def wait_block(h, w, i, leaf, size):
        rows = pl.ds(pl.multiple_of(i * R, R), size * R)
        block = wn.at[h, w, rows, :]
        pltpu.make_async_remote_copy(
            block, block, w_send.at[2], arrival(w, leaf, i),
            device_id=sibling, device_id_type=MESH).wait_recv()

    is_owner = functools.reduce(jnp.logical_or, [owns(w) for w in range(3)])
    owned_w = jnp.where(owns(0), 0, jnp.where(owns(1), 1, 2))

    def renew(i, targets):
        rows = slice(i * R, (i + 1) * R)
        old = w_ref[owned_w, rows, :].astype(F32)
        fresh = old - m_buf[rows, :].astype(F32)
        scale = jnp.sqrt(
            (jnp.mean(old * old, axis=1, keepdims=True) + 1e-06)
            / (jnp.mean(fresh * fresh, axis=1, keepdims=True) + 1e-06)
        )
        wn[y, owned_w, rows, :] = (fresh * scale).astype(BF16)
        w_copies(y, owned_w, i, targets)

    @pl.when(is_owner)
    def _():
        scale = 1.0 / (jnp.sqrt(jnp.sum(square[...])) + 1e-07)

        def mix(x_ref, factor):
            x = x_ref[...]
            g_buf[...] = (dot_nt(x, x) * factor).astype(BF16)
            g = g_buf[...]
            mix_buf[...] = (-4.775 * g.astype(F32) + 2.0315 * dot(g, g)).astype(BF16)

        mix(m_buf, scale * scale)
        m = m_buf[...]
        x_buf[...] = ((3.4445 * m.astype(F32) + dot(mix_buf[...], m)) * scale).astype(BF16)
        mix(x_buf, 1.0)
        edges = (
            (0, z < Z - 1, {"tok": me + 4}), (1, z > 0, {"tok": me - 4}),
            (3, True, across), (2, True, sibling),
        )
        step_rows = D // NS_BLOCKS
        for b in range(NS_BLOCKS):
            wide = slice(b * step_rows, (b + 1) * step_rows)
            m_buf[wide, :] = (
                3.4445 * x_buf[wide, :].astype(F32) + dot(mix_buf[wide, :], x_buf[...])
            ).astype(BF16)
            for i in range(b * CHUNKS // NS_BLOCKS, (b + 1) * CHUNKS // NS_BLOCKS):
                renew(i, edges)

    def spread_all(ws):
        routes = []
        end = 0
        for home in (True, False):
            h = y if home else 1 - y
            for w in ws:
                away = jnp.abs(z - owner_z(w, h))
                hops = away + (0 if home else 1)
                edge = jnp.logical_or(z == 0, z == Z - 1)
                start = LAG * jnp.maximum(away - 1, 0)
                if not home:
                    start = start + jnp.where(away > 0, jnp.where(edge, LEAF_END, LEAF), 0)
                routes.append((h, w, start, hops > 0, True, w_targets(w, home), not home))
                end = jnp.maximum(end, start + CHUNKS)
                if home and w == 1:
                    down = [(1, True, {"tok": me - 4})]
                    routes.append((h, w, start + LATE, z == 1, False, down, False))
                    end = jnp.maximum(end, start + LATE + CHUNKS)

        def step(t, _):
            for h, w, start, live, waits, targets, leaf in routes:
                i = t - start
                due = jnp.logical_and(i >= 0, i < CHUNKS)
                if leaf:
                    due = jnp.logical_and(due, i % 2 == 1)
                size = 2 if leaf else 1

                @pl.when(jnp.logical_and(live, due))
                def _():
                    if waits:
                        wait_block(h, w, i - (size - 1), leaf, size)
                    w_copies(h, w, i - (size - 1), targets, size)

            return 0

        lax.fori_loop(0, end, step, 0)

    @pl.when(pair)
    def _():
        spread_all((0, 1))

    @pl.when(jnp.logical_not(pair))
    def _():
        spread_all((2,))

    def save(h, w):
        return pltpu.make_async_copy(wn.at[h, w], neww_ref.at[h, w], out_sem.at[0])

    def save_all(ws):
        for w in ws:
            for h in range(HEADS):
                save(h, w).start()

    def finish(own, others):
        save_all(own)
        w_wait(wn.at[:, others[0] : others[-1] + 1], 2).wait_recv()
        save_all(others)

    @pl.when(pair)
    def _():
        finish((0, 1), (2,))

    @pl.when(jnp.logical_not(pair))
    def _():
        finish((2,), (0, 1))

    loads[4].wait()

    token_wait(1).wait_send()

    @pl.when(jnp.logical_or(jnp.logical_not(pair), middle))
    def _():
        token_wait(0).wait_send()

    @pl.when(jnp.logical_and(pair, middle))
    def _():
        token_wait(2).wait_send()

    for w in range(3):

        @pl.when(jnp.logical_and(pair, z != owner_z(w, y)))
        def _():
            chain_sent(w).wait_send()

    rise = jnp.where(pair, z < Z - 1, jnp.logical_and(z >= mid(y), z < Z - 1))
    fall = jnp.where(pair, z > 0, jnp.logical_and(z <= mid(y), z > 0))

    @pl.when(rise)
    def _():
        w_wait(wn.at[0, 0], 0).wait_send()

    @pl.when(fall)
    def _():
        w_wait(wn.at[0, 0], 1).wait_send()

    @pl.when(pair)
    def _():
        w_wait(wn.at[0, 0:2], 3).wait_send()
        w_wait(wn.at[:, 0:2], 2).wait_send()

    @pl.when(jnp.logical_not(pair))
    def _():
        w_wait(wn.at[0, 2], 3).wait_send()
        w_wait(wn.at[:, 2:3], 2).wait_send()

    pltpu.make_async_copy(wn, neww_ref, out_sem.at[0]).wait()


def readout(query_ref, w_ref, out, w_out, out_v, sem):
    copies = [
        pltpu.make_async_copy(w_ref, w_out, sem.at[0]),
        pltpu.make_async_copy(out_v, out, sem.at[1]),
    ]
    copies[0].start()
    D = w_ref.shape[2]
    for h in range(HEADS):
        cols = slice(h * D, (h + 1) * D)
        query = query_ref[:, cols]
        gate = dot(query, w_ref[h, 0])
        upper = dot(query, w_ref[h, 1])
        hidden = (gate * jax.nn.sigmoid(gate) * upper).astype(BF16)
        out_v[:, cols] = dot(hidden, w_ref[h, 2]).astype(BF16)
    copies[1].start()
    for cp in copies:
        cp.wait()


def body(Z, keys, values, queries, rates, fast_weights):
    D = fast_weights.shape[2]
    tokens = keys.shape[0]
    rows = tokens * 4
    vmem = pl.BlockSpec(memory_space=pltpu.VMEM)
    hbm = pl.BlockSpec(memory_space=pltpu.MemorySpace.HBM)

    def run(*refs):
        kernel(Z, *refs)

    query, fresh = pl.pallas_call(
        run,
        out_shape=(
            jax.ShapeDtypeStruct((tokens, HEADS * D), BF16),
            jax.ShapeDtypeStruct((HEADS, 3, D, D), BF16),
        ),
        in_specs=[hbm] * 5,
        out_specs=(pl.BlockSpec(memory_space=pl.ANY), pl.BlockSpec(memory_space=pl.ANY)),
        scratch_shapes=[
            pltpu.VMEM((tokens, HEADS * D), BF16),
            pltpu.VMEM(rates.shape, F32),
            pltpu.VMEM((3, D, D), BF16),
            pltpu.VMEM((HEADS, tokens, D), BF16),
            pltpu.VMEM((rows, D), BF16),
            pltpu.VMEM((rows, D), BF16),
            pltpu.VMEM((2, rows, D), F32),
            pltpu.VMEM((3, rows, D), BF16),
            pltpu.VMEM((3, D, D), F32),
            pltpu.VMEM((3, SUM_CHUNKS, D // SUM_CHUNKS, D), BF16),
            pltpu.VMEM((3, SUM_CHUNKS, D // SUM_CHUNKS, D), BF16),
            pltpu.VMEM((D // SUM_CHUNKS, D), F32),
            pltpu.VMEM((D, D), BF16),
            pltpu.VMEM((D, D), BF16),
            pltpu.VMEM((D, D), BF16),
            pltpu.VMEM((D, D), BF16),
            pltpu.VMEM((HEADS, 3, D, D), BF16),
            pltpu.SemaphoreType.DMA((3,)),
            pltpu.SemaphoreType.DMA((2, 4)),
            pltpu.SemaphoreType.DMA((3,)),
            pltpu.SemaphoreType.DMA((3, SUM_CHUNKS)),
            pltpu.SemaphoreType.DMA((4,)),
            pltpu.SemaphoreType.DMA((2, CHUNKS // 2)),
            pltpu.SemaphoreType.DMA((1,)),
            pltpu.SemaphoreType.DMA((1,)),
            pltpu.SemaphoreType.DMA((5,)),
        ],
        compiler_params=pltpu.CompilerParams(
            collective_id=0, has_side_effects=True, vmem_limit_bytes=30 * 1024 * 1024
        ),
        name="ttt_step",
    )(*[pltpu.with_memory_space_constraint(a, pltpu.MemorySpace.HBM) for a in (keys, values, queries, rates, fast_weights)])
    return pl.pallas_call(
        readout,
        out_shape=(
            jax.ShapeDtypeStruct(query.shape, BF16),
            jax.ShapeDtypeStruct(fresh.shape, BF16),
        ),
        in_specs=[vmem] * 2,
        out_specs=(hbm, hbm),
        scratch_shapes=[
            pltpu.VMEM(query.shape, BF16),
            pltpu.SemaphoreType.DMA((2,)),
        ],
        compiler_params=pltpu.CompilerParams(vmem_limit_bytes=4 * 1024 * 1024),
        name="readout",
    )(query, fresh)


def solution(mesh):
    Z = mesh.shape["tok"] // 4
    return jax.shard_map(
        functools.partial(body, Z),
        mesh=mesh,
        in_specs=(
            P(("grp", "tok"), None),
            P(("grp", "tok"), None),
            P(("grp", "tok"), None),
            P(None, ("grp", "tok")),
            P(),
        ),
        out_specs=(P(("grp", "tok"), None), P("grp", None, None, None)),
        check_vma=False,
    )
```

```python
import functools

import jax
import jax.numpy as jnp
from jax import lax
from jax.experimental import pallas as pl
from jax.experimental.pallas import tpu as pltpu
from jax.sharding import PartitionSpec as P

HEADS = 2
NS_BLOCKS = 4
CHUNKS = 16
SUM_CHUNKS = 16
SUM_LAG = 8
LAG = 5
LEAF = 16
LEAF_END = 8
LATE = 6
SHIFT = 0
MESH = pl.DeviceIdType.MESH
F32 = jnp.float32
BF16 = jnp.bfloat16


def dot(a, b):
    return jnp.dot(a, b, preferred_element_type=F32)


def dot_nt(a, b):
    return lax.dot_general(a, b, (((1,), (1,)), ((), ())), preferred_element_type=F32)


def dot_tn(a, b):
    return lax.dot_general(a, b, (((0,), (0,)), ((), ())), preferred_element_type=F32)


def kernel(
    Z,
    k_hbm, v_hbm, q_hbm, r_hbm, w_hbm,
    query_ref, neww_ref,
    v_ref, r_ref, w_ref,
    o_loc, keys, outer, gates, grads, sums, recv, sendbuf, square, m_buf, x_buf, g_buf, mix_buf, wn,
    tok_send, tok_recv, chain_send, chain_recv, w_send, w_recv, s_recv, out_sem, in_sem,
):
    tokens = k_hbm.shape[0]
    D = w_ref.shape[1]
    R = D // CHUNKS
    S = D // SUM_CHUNKS
    me = lax.axis_index("tok")
    c = me % 2
    y = (me // 2) % 2
    z = me // 4

    def mid(h):
        return Z // 2 - 1 + SHIFT * h

    def at(zz, yy, cc):
        return {"tok": (zz * 2 + yy) * 2 + cc}

    def block_rows(p):
        return pl.ds(pl.multiple_of(p * tokens, tokens), tokens)

    def head_cols(h):
        return pl.ds(pl.multiple_of(h * D, D), D)

    sibling = at(z, y, 1 - c)
    across = at(z, 1 - y, c)
    mine = y * 2 + c
    pair = c == 1
    gatherer = at(z, 1 - y, 1)
    middle = z == mid(y)
    sums_here = jnp.logical_or(pair, middle)

    barrier = pltpu.get_barrier_semaphore()
    for peer in (sibling, across, at(z, 1 - y, 1 - c)):
        pl.semaphore_signal(barrier, inc=1, device_id=peer, device_id_type=MESH)

    @pl.when(z > 0)
    def _():
        pl.semaphore_signal(barrier, inc=1, device_id={"tok": me - 4}, device_id_type=MESH)

    @pl.when(z < Z - 1)
    def _():
        pl.semaphore_signal(barrier, inc=1, device_id={"tok": me + 4}, device_id_type=MESH)

    loads = [
        pltpu.make_async_copy(src, dst, in_sem.at[n])
        for n, (src, dst) in enumerate((
            (r_hbm, r_ref), (v_hbm, v_ref),
            (k_hbm.at[:, head_cols(y)], keys.at[block_rows(mine), :]),
            (w_hbm.at[y], w_ref), (q_hbm, query_ref),
        ))
    ]
    for load in loads:
        load.start()
    square[...] = jnp.zeros_like(square)

    def token_copy(a, kind):
        h = y if kind == 0 else 1 - y
        src = o_loc.at[h] if a else k_hbm.at[:, head_cols(h)]
        return pltpu.make_async_remote_copy(
            src, (keys, outer)[a].at[block_rows(mine), :],
            tok_send.at[kind], tok_recv.at[a, mine],
            device_id=gatherer if kind else sibling, device_id_type=MESH)

    def pass_on(a, p):
        block = (keys, outer)[a].at[block_rows(p), :]
        return pltpu.make_async_remote_copy(
            block, block, tok_send.at[2], tok_recv.at[a, p],
            device_id=sibling, device_id_type=MESH)

    def token_wait(kind):
        block = keys.at[pl.ds(0, tokens * (4 if kind == 2 else 2)), :]
        return pltpu.make_async_remote_copy(
            block, block, tok_send.at[kind], tok_recv.at[0, 0],
            device_id=sibling, device_id_type=MESH)

    def send_tokens(a):
        token_copy(a, 1).start()

        @pl.when(jnp.logical_or(jnp.logical_not(pair), middle))
        def _():
            token_copy(a, 0).start()

    pl.semaphore_wait(barrier, 3 + jnp.where(z > 0, 1, 0) + jnp.where(z < Z - 1, 1, 0))
    send_tokens(0)
    loads[0].wait()
    loads[1].wait()
    for h in range(HEADS):
        row = jnp.broadcast_to(r_ref[h : h + 1, :], (128, tokens))
        col = jnp.concatenate([row.T] * (D // 128), axis=1)
        o_loc[h] = (-col * v_ref[:, h * D : (h + 1) * D].astype(F32)).astype(BF16)

    send_tokens(1)
    outer[block_rows(mine), :] = o_loc[y]
    loads[2].wait()
    loads[3].wait()

    def forward_step(s, _):
        d = s // 4 * 2 + s % 2
        p = jnp.where(d < 2, y * 2 + jnp.where(d == 0, c, 1 - c), (1 - y) * 2 + d % 2)
        rows = block_rows(p)
        for a in range(2):

            @pl.when(jnp.logical_and(s // 2 % 2 == a, d > 0))
            def _():
                pass_on(a, p).wait_recv()

                @pl.when(jnp.logical_and(jnp.logical_and(pair, middle), d >= 2))
                def _():
                    pass_on(a, p).start()

        @pl.when(s // 2 % 2 == 0)
        def _():
            key = keys[rows, :]
            gate = dot(key, w_ref[0])
            upper = dot(key, w_ref[1])

            sigma = jax.nn.sigmoid(gate)
            silu_gate = gate * sigma
            gates[0, rows, :] = upper * sigma * (1.0 + gate * (1.0 - sigma))
            gates[1, rows, :] = silu_gate
            grads[2, rows, :] = (silu_gate * upper).astype(BF16)

        @pl.when(jnp.logical_and(pair, s // 2 % 2 == 1))
        def _():
            back = dot_nt(outer[rows, :], w_ref[2])
            grads[0, rows, :] = (back * gates[0, rows, :]).astype(BF16)
            grads[1, rows, :] = (back * gates[1, rows, :]).astype(BF16)

        return 0

    lax.fori_loop(0, jnp.where(sums_here, 8, 0), forward_step, 0)

    def owner_z(w, h):
        return (0, Z - 1, mid(h))[w]

    def chain_copy(w, i, step, side):
        there = z + step == mid(y)
        held = jnp.where(there, side, 2) if w == 2 else w
        core = jnp.where(there, 0, 1) if w == 2 else 1
        return pltpu.make_async_remote_copy(
            sendbuf.at[w, i], recv.at[held, i], chain_send.at[w], chain_recv.at[held, i],
            device_id=at(z + step, y, core), device_id_type=MESH)

    def chain_sent(w):
        block = sendbuf.at[w]
        return pltpu.make_async_remote_copy(
            block, block, chain_send.at[w], chain_recv.at[w, 0],
            device_id=sibling, device_id_type=MESH)

    def chain_roles(w):
        own = owner_z(w, y)
        return (
            jnp.logical_and(z > 0, z <= own), jnp.logical_and(z < Z - 1, z >= own),
            z == own, z < own, z > own,
        )

    def reduce_event(w, i, roles):
        below, above, ends, rises, falls = roles
        rows = pl.ds(pl.multiple_of(i * S, S), S)

        def take(side):
            held = jnp.where(middle, side, 2) if w == 2 else w
            block = recv.at[held, i]
            pltpu.make_async_remote_copy(
                block, block, chain_send.at[w], chain_recv.at[held, i],
                device_id=sibling, device_id_type=MESH).wait_recv()
            sums[w, rows, :] += recv[held, i].astype(F32)

        @pl.when(below)
        def _():
            take(0)

        @pl.when(above)
        def _():
            take(1)

        @pl.when(ends)
        def _():
            rounded = sums[w, rows, :].astype(BF16)
            m_buf[rows, :] = rounded
            square[...] += jnp.square(rounded.astype(F32))

        @pl.when(jnp.logical_not(ends))
        def _():
            sendbuf[w, i] = sums[w, rows, :].astype(BF16)

        @pl.when(rises)
        def _():
            chain_copy(w, i, 1, 0).start()

        @pl.when(falls)
        def _():
            chain_copy(w, i, -1, 1).start()

    def depth(w):
        own = owner_z(w, y)
        rise = jnp.where(z <= own, z, 0)
        fall = jnp.where(z >= own, Z - 1 - z, 0)
        return SUM_LAG * jnp.maximum(rise, fall)

    def reduce_all(ws, depths, live):
        roles = [chain_roles(w) for w in ws]

        def step(t, _):
            for w, lag, role, on in zip(ws, depths, roles, live):
                i = t - lag

                @pl.when(jnp.logical_and(on, jnp.logical_and(i >= 0, i < SUM_CHUNKS)))
                def _():
                    reduce_event(w, i, role)

            return 0

        return step

    @pl.when(pair)
    def _():
        depths = [depth(0), depth(1), depth(2) + SUM_CHUNKS]
        step = reduce_all((0, 1, 2), depths, (True, True, jnp.logical_not(middle)))
        near = jnp.where(2 * z < Z, 1, 0)
        edge = jnp.logical_or(z == 0, z == Z - 1)
        first = jnp.where(edge, SUM_CHUNKS, 0)

        def near_part(n, _):
            rows = pl.ds(pl.multiple_of(n * (D // 4), D // 4), D // 4)
            sums[near, rows, :] = dot_tn(keys[:, rows], grads[near])
            lax.fori_loop(first * n // 4, first * (n + 1) // 4, step, 0)
            return 0

        lax.fori_loop(0, 4, near_part, 0)
        sums[1 - near] = dot_tn(keys[...], grads[1 - near])
        sums[2] = dot_tn(grads[2], outer[...])
        lax.fori_loop(first, SUM_CHUNKS + functools.reduce(jnp.maximum, depths), step, 0)

    @pl.when(jnp.logical_and(jnp.logical_not(pair), middle))
    def _():
        sums[2] = dot_tn(grads[2], outer[...])
        lax.fori_loop(0, SUM_CHUNKS, reduce_all((2,), (0,), (True,)), 0)

    def owns(w):
        return jnp.logical_and(pair == (w < 2), z == owner_z(w, y))

    def w_targets(w, home):
        own = owner_z(w, y)
        leaf = (2, True, sibling)
        if not home:
            return (leaf,)
        return (
            (0, jnp.logical_and(z >= own, z < Z - 1), {"tok": me + 4}),
            (1, jnp.logical_and(z <= own, z > (1 if w == 1 else 0)), {"tok": me - 4}),
            (3, True, across),
            leaf,
        )

    def arrival(w, leaf, i):
        return w_recv.at[w % 2, i // 2] if leaf else chain_recv.at[w % 2, i]

    def w_copies(h, w, i, targets, size=1):
        rows = pl.ds(pl.multiple_of(i * R, R), size * R)
        block = wn.at[h, w, rows, :]

        def copy(kind, dev):
            pltpu.make_async_remote_copy(
                block, block, w_send.at[kind],
                arrival(w, kind == 3, i) if kind != 2 else s_recv.at[0],
                device_id=dev, device_id_type=MESH).start()

        for kind, go, dev in targets:
            if go is True:
                copy(kind, dev)
            else:

                @pl.when(go)
                def _():
                    copy(kind, dev)

    def w_wait(block, kind):
        return pltpu.make_async_remote_copy(
            block, block, w_send.at[kind], s_recv.at[0],
            device_id=sibling, device_id_type=MESH)

    def wait_block(h, w, i, leaf, size):
        rows = pl.ds(pl.multiple_of(i * R, R), size * R)
        block = wn.at[h, w, rows, :]
        pltpu.make_async_remote_copy(
            block, block, w_send.at[2], arrival(w, leaf, i),
            device_id=sibling, device_id_type=MESH).wait_recv()

    is_owner = functools.reduce(jnp.logical_or, [owns(w) for w in range(3)])
    owned_w = jnp.where(owns(0), 0, jnp.where(owns(1), 1, 2))

    def renew(i, targets):
        rows = slice(i * R, (i + 1) * R)
        old = w_ref[owned_w, rows, :].astype(F32)
        fresh = old - m_buf[rows, :].astype(F32)
        scale = jnp.sqrt(
            (jnp.mean(old * old, axis=1, keepdims=True) + 1e-06)
            / (jnp.mean(fresh * fresh, axis=1, keepdims=True) + 1e-06)
        )
        wn[y, owned_w, rows, :] = (fresh * scale).astype(BF16)
        w_copies(y, owned_w, i, targets)

    @pl.when(is_owner)
    def _():
        scale = 1.0 / (jnp.sqrt(jnp.sum(square[...])) + 1e-07)

        def mix(x_ref, factor):
            x = x_ref[...]
            g_buf[...] = (dot_nt(x, x) * factor).astype(BF16)
            g = g_buf[...]
            mix_buf[...] = (-4.775 * g.astype(F32) + 2.0315 * dot(g, g)).astype(BF16)

        mix(m_buf, scale * scale)
        m = m_buf[...]
        x_buf[...] = ((3.4445 * m.astype(F32) + dot(mix_buf[...], m)) * scale).astype(BF16)
        mix(x_buf, 1.0)
        edges = (
            (0, z < Z - 1, {"tok": me + 4}), (1, z > 0, {"tok": me - 4}),
            (3, True, across), (2, True, sibling),
        )
        step_rows = D // NS_BLOCKS
        for b in range(NS_BLOCKS):
            wide = slice(b * step_rows, (b + 1) * step_rows)
            m_buf[wide, :] = (
                3.4445 * x_buf[wide, :].astype(F32) + dot(mix_buf[wide, :], x_buf[...])
            ).astype(BF16)
            for i in range(b * CHUNKS // NS_BLOCKS, (b + 1) * CHUNKS // NS_BLOCKS):
                renew(i, edges)

    def spread_all(ws):
        routes = []
        end = 0
        for home in (True, False):
            h = y if home else 1 - y
            for w in ws:
                away = jnp.abs(z - owner_z(w, h))
                hops = away + (0 if home else 1)
                edge = jnp.logical_or(z == 0, z == Z - 1)
                start = LAG * jnp.maximum(away - 1, 0)
                if not home:
                    start = start + jnp.where(away > 0, jnp.where(edge, LEAF_END, LEAF), 0)
                routes.append((h, w, start, hops > 0, True, w_targets(w, home), not home))
                end = jnp.maximum(end, start + CHUNKS)
                if home and w == 1:
                    down = [(1, True, {"tok": me - 4})]
                    routes.append((h, w, start + LATE, z == 1, False, down, False))
                    end = jnp.maximum(end, start + LATE + CHUNKS)

        def step(t, _):
            for h, w, start, live, waits, targets, leaf in routes:
                i = t - start
                due = jnp.logical_and(i >= 0, i < CHUNKS)
                if leaf:
                    due = jnp.logical_and(due, i % 2 == 1)
                size = 2 if leaf else 1

                @pl.when(jnp.logical_and(live, due))
                def _():
                    if waits:
                        wait_block(h, w, i - (size - 1), leaf, size)
                    w_copies(h, w, i - (size - 1), targets, size)

            return 0

        lax.fori_loop(0, end, step, 0)

    @pl.when(pair)
    def _():
        spread_all((0, 1))

    @pl.when(jnp.logical_not(pair))
    def _():
        spread_all((2,))

    def save(h, w):
        return pltpu.make_async_copy(wn.at[h, w], neww_ref.at[h, w], out_sem.at[0])

    def save_all(ws):
        for w in ws:
            for h in range(HEADS):
                save(h, w).start()

    def finish(own, others):
        save_all(own)
        w_wait(wn.at[:, others[0] : others[-1] + 1], 2).wait_recv()
        save_all(others)

    @pl.when(pair)
    def _():
        finish((0, 1), (2,))

    @pl.when(jnp.logical_not(pair))
    def _():
        finish((2,), (0, 1))

    loads[4].wait()

    token_wait(1).wait_send()

    @pl.when(jnp.logical_or(jnp.logical_not(pair), middle))
    def _():
        token_wait(0).wait_send()

    @pl.when(jnp.logical_and(pair, middle))
    def _():
        token_wait(2).wait_send()

    for w in range(3):

        @pl.when(jnp.logical_and(pair, z != owner_z(w, y)))
        def _():
            chain_sent(w).wait_send()

    rise = jnp.where(pair, z < Z - 1, jnp.logical_and(z >= mid(y), z < Z - 1))
    fall = jnp.where(pair, z > 0, jnp.logical_and(z <= mid(y), z > 0))

    @pl.when(rise)
    def _():
        w_wait(wn.at[0, 0], 0).wait_send()

    @pl.when(fall)
    def _():
        w_wait(wn.at[0, 0], 1).wait_send()

    @pl.when(pair)
    def _():
        w_wait(wn.at[0, 0:2], 3).wait_send()
        w_wait(wn.at[:, 0:2], 2).wait_send()

    @pl.when(jnp.logical_not(pair))
    def _():
        w_wait(wn.at[0, 2], 3).wait_send()
        w_wait(wn.at[:, 2:3], 2).wait_send()

    pltpu.make_async_copy(wn, neww_ref, out_sem.at[0]).wait()


def readout(query_ref, w_ref, out, w_out, out_v, sem):
    copies = [
        pltpu.make_async_copy(w_ref, w_out, sem.at[0]),
        pltpu.make_async_copy(out_v, out, sem.at[1]),
    ]
    copies[0].start()
    D = w_ref.shape[2]
    for h in range(HEADS):
        cols = slice(h * D, (h + 1) * D)
        query = query_ref[:, cols]
        gate = dot(query, w_ref[h, 0])
        upper = dot(query, w_ref[h, 1])
        hidden = (gate * jax.nn.sigmoid(gate) * upper).astype(BF16)
        out_v[:, cols] = dot(hidden, w_ref[h, 2]).astype(BF16)
    copies[1].start()
    for cp in copies:
        cp.wait()


def body(Z, keys, values, queries, rates, fast_weights):
    D = fast_weights.shape[2]
    tokens = keys.shape[0]
    rows = tokens * 4
    vmem = pl.BlockSpec(memory_space=pltpu.VMEM)
    hbm = pl.BlockSpec(memory_space=pltpu.MemorySpace.HBM)

    def run(*refs):
        kernel(Z, *refs)

    query, fresh = pl.pallas_call(
        run,
        out_shape=(
            jax.ShapeDtypeStruct((tokens, HEADS * D), BF16),
            jax.ShapeDtypeStruct((HEADS, 3, D, D), BF16),
        ),
        in_specs=[hbm] * 5,
        out_specs=(pl.BlockSpec(memory_space=pl.ANY), pl.BlockSpec(memory_space=pl.ANY)),
        scratch_shapes=[
            pltpu.VMEM((tokens, HEADS * D), BF16),
            pltpu.VMEM(rates.shape, F32),
            pltpu.VMEM((3, D, D), BF16),
            pltpu.VMEM((HEADS, tokens, D), BF16),
            pltpu.VMEM((rows, D), BF16),
            pltpu.VMEM((rows, D), BF16),
            pltpu.VMEM((2, rows, D), F32),
            pltpu.VMEM((3, rows, D), BF16),
            pltpu.VMEM((3, D, D), F32),
            pltpu.VMEM((3, SUM_CHUNKS, D // SUM_CHUNKS, D), BF16),
            pltpu.VMEM((3, SUM_CHUNKS, D // SUM_CHUNKS, D), BF16),
            pltpu.VMEM((D // SUM_CHUNKS, D), F32),
            pltpu.VMEM((D, D), BF16),
            pltpu.VMEM((D, D), BF16),
            pltpu.VMEM((D, D), BF16),
            pltpu.VMEM((D, D), BF16),
            pltpu.VMEM((HEADS, 3, D, D), BF16),
            pltpu.SemaphoreType.DMA((3,)),
            pltpu.SemaphoreType.DMA((2, 4)),
            pltpu.SemaphoreType.DMA((3,)),
            pltpu.SemaphoreType.DMA((3, SUM_CHUNKS)),
            pltpu.SemaphoreType.DMA((4,)),
            pltpu.SemaphoreType.DMA((2, CHUNKS // 2)),
            pltpu.SemaphoreType.DMA((1,)),
            pltpu.SemaphoreType.DMA((1,)),
            pltpu.SemaphoreType.DMA((5,)),
        ],
        compiler_params=pltpu.CompilerParams(
            collective_id=0, has_side_effects=True, vmem_limit_bytes=30 * 1024 * 1024
        ),
        name="ttt_step",
    )(*[pltpu.with_memory_space_constraint(a, pltpu.MemorySpace.HBM) for a in (keys, values, queries, rates, fast_weights)])
    return pl.pallas_call(
        readout,
        out_shape=(
            jax.ShapeDtypeStruct(query.shape, BF16),
            jax.ShapeDtypeStruct(fresh.shape, BF16),
        ),
        in_specs=[vmem] * 2,
        out_specs=(hbm, hbm),
        scratch_shapes=[
            pltpu.VMEM(query.shape, BF16),
            pltpu.SemaphoreType.DMA((2,)),
        ],
        compiler_params=pltpu.CompilerParams(vmem_limit_bytes=4 * 1024 * 1024),
        name="readout",
    )(query, fresh)


def solution(mesh):
    Z = mesh.shape["tok"] // 4
    return jax.shard_map(
        functools.partial(body, Z),
        mesh=mesh,
        in_specs=(
            P(("grp", "tok"), None),
            P(("grp", "tok"), None),
            P(("grp", "tok"), None),
            P(None, ("grp", "tok")),
            P(),
        ),
        out_specs=(P(("grp", "tok"), None), P("grp", None, None, None)),
        check_vma=False,
    )
```

```python
import functools

import jax
import jax.numpy as jnp
from jax import lax
from jax.experimental import pallas as pl
from jax.experimental.pallas import tpu as pltpu
from jax.sharding import PartitionSpec as P

HEADS = 2
NS_BLOCKS = 4
CHUNKS = 16
SUM_CHUNKS = 16
SUM_LAG = 7
LAG = 6
LEAF = 16
LEAF_END = 8
LATE = 4
SHIFT = 0
MESH = pl.DeviceIdType.MESH
F32 = jnp.float32
BF16 = jnp.bfloat16


def dot(a, b):
    return jnp.dot(a, b, preferred_element_type=F32)


def dot_nt(a, b):
    return lax.dot_general(a, b, (((1,), (1,)), ((), ())), preferred_element_type=F32)


def dot_tn(a, b):
    return lax.dot_general(a, b, (((0,), (0,)), ((), ())), preferred_element_type=F32)


def kernel(
    Z,
    k_hbm, v_hbm, q_hbm, r_hbm, w_hbm,
    query_ref, neww_ref,
    v_ref, r_ref, w_ref,
    o_loc, keys, outer, gates, grads, sums, recv, sendbuf, square, m_buf, x_buf, g_buf, mix_buf, wn,
    tok_send, tok_recv, chain_send, chain_recv, w_send, w_recv, s_recv, out_sem, in_sem,
):
    tokens = k_hbm.shape[0]
    D = w_ref.shape[1]
    R = D // CHUNKS
    S = D // SUM_CHUNKS
    me = lax.axis_index("tok")
    c = me % 2
    y = (me // 2) % 2
    z = me // 4

    def mid(h):
        return Z // 2 - 1 + SHIFT * h

    def at(zz, yy, cc):
        return {"tok": (zz * 2 + yy) * 2 + cc}

    def block_rows(p):
        return pl.ds(pl.multiple_of(p * tokens, tokens), tokens)

    def head_cols(h):
        return pl.ds(pl.multiple_of(h * D, D), D)

    sibling = at(z, y, 1 - c)
    across = at(z, 1 - y, c)
    mine = y * 2 + c
    pair = c == 1
    gatherer = at(z, 1 - y, 1)
    middle = z == mid(y)
    sums_here = jnp.logical_or(pair, middle)

    barrier = pltpu.get_barrier_semaphore()
    for peer in (sibling, across, at(z, 1 - y, 1 - c)):
        pl.semaphore_signal(barrier, inc=1, device_id=peer, device_id_type=MESH)

    @pl.when(z > 0)
    def _():
        pl.semaphore_signal(barrier, inc=1, device_id={"tok": me - 4}, device_id_type=MESH)

    @pl.when(z < Z - 1)
    def _():
        pl.semaphore_signal(barrier, inc=1, device_id={"tok": me + 4}, device_id_type=MESH)

    loads = [
        pltpu.make_async_copy(src, dst, in_sem.at[n])
        for n, (src, dst) in enumerate((
            (r_hbm, r_ref), (v_hbm, v_ref),
            (k_hbm.at[:, head_cols(y)], keys.at[block_rows(mine), :]),
            (w_hbm.at[y], w_ref), (q_hbm, query_ref),
        ))
    ]
    for load in loads:
        load.start()
    square[...] = jnp.zeros_like(square)

    def token_copy(a, kind):
        h = y if kind == 0 else 1 - y
        src = o_loc.at[h] if a else k_hbm.at[:, head_cols(h)]
        return pltpu.make_async_remote_copy(
            src, (keys, outer)[a].at[block_rows(mine), :],
            tok_send.at[kind], tok_recv.at[a, mine],
            device_id=gatherer if kind else sibling, device_id_type=MESH)

    def pass_on(a, p):
        block = (keys, outer)[a].at[block_rows(p), :]
        return pltpu.make_async_remote_copy(
            block, block, tok_send.at[2], tok_recv.at[a, p],
            device_id=sibling, device_id_type=MESH)

    def token_wait(kind):
        block = keys.at[pl.ds(0, tokens * (4 if kind == 2 else 2)), :]
        return pltpu.make_async_remote_copy(
            block, block, tok_send.at[kind], tok_recv.at[0, 0],
            device_id=sibling, device_id_type=MESH)

    def send_tokens(a):
        token_copy(a, 1).start()

        @pl.when(jnp.logical_or(jnp.logical_not(pair), middle))
        def _():
            token_copy(a, 0).start()

    pl.semaphore_wait(barrier, 3 + jnp.where(z > 0, 1, 0) + jnp.where(z < Z - 1, 1, 0))
    send_tokens(0)
    loads[0].wait()
    loads[1].wait()
    for h in range(HEADS):
        row = jnp.broadcast_to(r_ref[h : h + 1, :], (128, tokens))
        col = jnp.concatenate([row.T] * (D // 128), axis=1)
        o_loc[h] = (-col * v_ref[:, h * D : (h + 1) * D].astype(F32)).astype(BF16)

    send_tokens(1)
    outer[block_rows(mine), :] = o_loc[y]
    loads[2].wait()
    loads[3].wait()

    def forward_step(s, _):
        d = s // 4 * 2 + s % 2
        p = jnp.where(d < 2, y * 2 + jnp.where(d == 0, c, 1 - c), (1 - y) * 2 + d % 2)
        rows = block_rows(p)
        for a in range(2):

            @pl.when(jnp.logical_and(s // 2 % 2 == a, d > 0))
            def _():
                pass_on(a, p).wait_recv()

                @pl.when(jnp.logical_and(jnp.logical_and(pair, middle), d >= 2))
                def _():
                    pass_on(a, p).start()

        @pl.when(s // 2 % 2 == 0)
        def _():
            key = keys[rows, :]
            gate = dot(key, w_ref[0])
            upper = dot(key, w_ref[1])

            sigma = jax.nn.sigmoid(gate)
            silu_gate = gate * sigma
            gates[0, rows, :] = upper * sigma * (1.0 + gate * (1.0 - sigma))
            gates[1, rows, :] = silu_gate
            grads[2, rows, :] = (silu_gate * upper).astype(BF16)

        @pl.when(jnp.logical_and(pair, s // 2 % 2 == 1))
        def _():
            back = dot_nt(outer[rows, :], w_ref[2])
            grads[0, rows, :] = (back * gates[0, rows, :]).astype(BF16)
            grads[1, rows, :] = (back * gates[1, rows, :]).astype(BF16)

        return 0

    lax.fori_loop(0, jnp.where(sums_here, 8, 0), forward_step, 0)

    def owner_z(w, h):
        return (0, Z - 1, mid(h))[w]

    def chain_copy(w, i, step, side):
        there = z + step == mid(y)
        held = jnp.where(there, side, 2) if w == 2 else w
        core = jnp.where(there, 0, 1) if w == 2 else 1
        return pltpu.make_async_remote_copy(
            sendbuf.at[w, i], recv.at[held, i], chain_send.at[w], chain_recv.at[held, i],
            device_id=at(z + step, y, core), device_id_type=MESH)

    def chain_sent(w):
        block = sendbuf.at[w]
        return pltpu.make_async_remote_copy(
            block, block, chain_send.at[w], chain_recv.at[w, 0],
            device_id=sibling, device_id_type=MESH)

    def chain_roles(w):
        own = owner_z(w, y)
        return (
            jnp.logical_and(z > 0, z <= own), jnp.logical_and(z < Z - 1, z >= own),
            z == own, z < own, z > own,
        )

    def reduce_event(w, i, roles):
        below, above, ends, rises, falls = roles
        rows = pl.ds(pl.multiple_of(i * S, S), S)

        def take(side):
            held = jnp.where(middle, side, 2) if w == 2 else w
            block = recv.at[held, i]
            pltpu.make_async_remote_copy(
                block, block, chain_send.at[w], chain_recv.at[held, i],
                device_id=sibling, device_id_type=MESH).wait_recv()
            sums[w, rows, :] += recv[held, i].astype(F32)

        @pl.when(below)
        def _():
            take(0)

        @pl.when(above)
        def _():
            take(1)

        @pl.when(ends)
        def _():
            rounded = sums[w, rows, :].astype(BF16)
            m_buf[rows, :] = rounded
            square[...] += jnp.square(rounded.astype(F32))

        @pl.when(jnp.logical_not(ends))
        def _():
            sendbuf[w, i] = sums[w, rows, :].astype(BF16)

        @pl.when(rises)
        def _():
            chain_copy(w, i, 1, 0).start()

        @pl.when(falls)
        def _():
            chain_copy(w, i, -1, 1).start()

    def depth(w):
        own = owner_z(w, y)
        rise = jnp.where(z <= own, z, 0)
        fall = jnp.where(z >= own, Z - 1 - z, 0)
        return SUM_LAG * jnp.maximum(rise, fall)

    def reduce_all(ws, depths, live):
        roles = [chain_roles(w) for w in ws]

        def step(t, _):
            for w, lag, role, on in zip(ws, depths, roles, live):
                i = t - lag

                @pl.when(jnp.logical_and(on, jnp.logical_and(i >= 0, i < SUM_CHUNKS)))
                def _():
                    reduce_event(w, i, role)

            return 0

        return step

    @pl.when(pair)
    def _():
        depths = [depth(0), depth(1), depth(2) + SUM_CHUNKS]
        step = reduce_all((0, 1, 2), depths, (True, True, jnp.logical_not(middle)))
        near = jnp.where(2 * z < Z, 1, 0)
        edge = jnp.logical_or(z == 0, z == Z - 1)
        first = jnp.where(edge, SUM_CHUNKS, 0)

        def near_part(n, _):
            rows = pl.ds(pl.multiple_of(n * (D // 4), D // 4), D // 4)
            sums[near, rows, :] = dot_tn(keys[:, rows], grads[near])
            lax.fori_loop(first * n // 4, first * (n + 1) // 4, step, 0)
            return 0

        lax.fori_loop(0, 4, near_part, 0)
        sums[1 - near] = dot_tn(keys[...], grads[1 - near])
        sums[2] = dot_tn(grads[2], outer[...])
        lax.fori_loop(first, SUM_CHUNKS + functools.reduce(jnp.maximum, depths), step, 0)

    @pl.when(jnp.logical_and(jnp.logical_not(pair), middle))
    def _():
        sums[2] = dot_tn(grads[2], outer[...])
        lax.fori_loop(0, SUM_CHUNKS, reduce_all((2,), (0,), (True,)), 0)

    def owns(w):
        return jnp.logical_and(pair == (w < 2), z == owner_z(w, y))

    def w_targets(w, home):
        own = owner_z(w, y)
        leaf = (2, True, sibling)
        if not home:
            return (leaf,)
        return (
            (3, True, across),
            (0, jnp.logical_and(z >= own, z < Z - 1), {"tok": me + 4}),
            (1, jnp.logical_and(z <= own, z > (1 if w == 1 else 0)), {"tok": me - 4}),
            leaf,
        )

    def arrival(w, leaf, i):
        return w_recv.at[w % 2, i // 2] if leaf else chain_recv.at[w % 2, i]

    def w_copies(h, w, i, targets, size=1):
        rows = pl.ds(pl.multiple_of(i * R, R), size * R)
        block = wn.at[h, w, rows, :]

        def copy(kind, dev):
            pltpu.make_async_remote_copy(
                block, block, w_send.at[kind],
                arrival(w, kind == 3, i) if kind != 2 else s_recv.at[0],
                device_id=dev, device_id_type=MESH).start()

        for kind, go, dev in targets:
            if go is True:
                copy(kind, dev)
            else:

                @pl.when(go)
                def _():
                    copy(kind, dev)

    def w_wait(block, kind):
        return pltpu.make_async_remote_copy(
            block, block, w_send.at[kind], s_recv.at[0],
            device_id=sibling, device_id_type=MESH)

    def wait_block(h, w, i, leaf, size):
        rows = pl.ds(pl.multiple_of(i * R, R), size * R)
        block = wn.at[h, w, rows, :]
        pltpu.make_async_remote_copy(
            block, block, w_send.at[2], arrival(w, leaf, i),
            device_id=sibling, device_id_type=MESH).wait_recv()

    is_owner = functools.reduce(jnp.logical_or, [owns(w) for w in range(3)])
    owned_w = jnp.where(owns(0), 0, jnp.where(owns(1), 1, 2))

    def renew(i, targets):
        rows = slice(i * R, (i + 1) * R)
        old = w_ref[owned_w, rows, :].astype(F32)
        fresh = old - m_buf[rows, :].astype(F32)
        scale = jnp.sqrt(
            (jnp.mean(old * old, axis=1, keepdims=True) + 1e-06)
            / (jnp.mean(fresh * fresh, axis=1, keepdims=True) + 1e-06)
        )
        wn[y, owned_w, rows, :] = (fresh * scale).astype(BF16)
        w_copies(y, owned_w, i, targets)

    @pl.when(is_owner)
    def _():
        scale = 1.0 / (jnp.sqrt(jnp.sum(square[...])) + 1e-07)

        def mix(x_ref, factor):
            x = x_ref[...]
            g_buf[...] = (dot_nt(x, x) * factor).astype(BF16)
            g = g_buf[...]
            mix_buf[...] = (-4.775 * g.astype(F32) + 2.0315 * dot(g, g)).astype(BF16)

        mix(m_buf, scale * scale)
        m = m_buf[...]
        x_buf[...] = ((3.4445 * m.astype(F32) + dot(mix_buf[...], m)) * scale).astype(BF16)
        mix(x_buf, 1.0)
        edges = (
            (3, True, across), (0, z < Z - 1, {"tok": me + 4}),
            (1, z > 0, {"tok": me - 4}), (2, True, sibling),
        )
        step_rows = D // NS_BLOCKS
        for b in range(NS_BLOCKS):
            wide = slice(b * step_rows, (b + 1) * step_rows)
            m_buf[wide, :] = (
                3.4445 * x_buf[wide, :].astype(F32) + dot(mix_buf[wide, :], x_buf[...])
            ).astype(BF16)
            for i in range(b * CHUNKS // NS_BLOCKS, (b + 1) * CHUNKS // NS_BLOCKS):
                renew(i, edges)

    def spread_all(ws):
        routes = []
        end = 0
        for home in (True, False):
            h = y if home else 1 - y
            for w in ws:
                away = jnp.abs(z - owner_z(w, h))
                hops = away + (0 if home else 1)
                edge = jnp.logical_or(z == 0, z == Z - 1)
                start = LAG * jnp.maximum(away - 1, 0)
                if not home:
                    start = start + jnp.where(away > 0, jnp.where(edge, LEAF_END, LEAF), 0)
                routes.append((h, w, start, hops > 0, True, w_targets(w, home), not home))
                end = jnp.maximum(end, start + CHUNKS)
                if home and w == 1:
                    down = [(1, True, {"tok": me - 4})]
                    routes.append((h, w, start + LATE, z == 1, False, down, False))
                    end = jnp.maximum(end, start + LATE + CHUNKS)

        def step(t, _):
            for h, w, start, live, waits, targets, leaf in routes:
                i = t - start
                due = jnp.logical_and(i >= 0, i < CHUNKS)
                if leaf:
                    due = jnp.logical_and(due, i % 2 == 1)
                size = 2 if leaf else 1

                @pl.when(jnp.logical_and(live, due))
                def _():
                    if waits:
                        wait_block(h, w, i - (size - 1), leaf, size)
                    w_copies(h, w, i - (size - 1), targets, size)

            return 0

        lax.fori_loop(0, end, step, 0)

    @pl.when(pair)
    def _():
        spread_all((0, 1))

    @pl.when(jnp.logical_not(pair))
    def _():
        spread_all((2,))

    def save(h, w):
        return pltpu.make_async_copy(wn.at[h, w], neww_ref.at[h, w], out_sem.at[0])

    def save_all(ws):
        for w in ws:
            for h in range(HEADS):
                save(h, w).start()

    def finish(own, others):
        save_all(own)
        w_wait(wn.at[:, others[0] : others[-1] + 1], 2).wait_recv()
        save_all(others)

    @pl.when(pair)
    def _():
        finish((0, 1), (2,))

    @pl.when(jnp.logical_not(pair))
    def _():
        finish((2,), (0, 1))

    loads[4].wait()

    token_wait(1).wait_send()

    @pl.when(jnp.logical_or(jnp.logical_not(pair), middle))
    def _():
        token_wait(0).wait_send()

    @pl.when(jnp.logical_and(pair, middle))
    def _():
        token_wait(2).wait_send()

    for w in range(3):

        @pl.when(jnp.logical_and(pair, z != owner_z(w, y)))
        def _():
            chain_sent(w).wait_send()

    rise = jnp.where(pair, z < Z - 1, jnp.logical_and(z >= mid(y), z < Z - 1))
    fall = jnp.where(pair, z > 0, jnp.logical_and(z <= mid(y), z > 0))

    @pl.when(rise)
    def _():
        w_wait(wn.at[0, 0], 0).wait_send()

    @pl.when(fall)
    def _():
        w_wait(wn.at[0, 0], 1).wait_send()

    @pl.when(pair)
    def _():
        w_wait(wn.at[0, 0:2], 3).wait_send()
        w_wait(wn.at[:, 0:2], 2).wait_send()

    @pl.when(jnp.logical_not(pair))
    def _():
        w_wait(wn.at[0, 2], 3).wait_send()
        w_wait(wn.at[:, 2:3], 2).wait_send()

    pltpu.make_async_copy(wn, neww_ref, out_sem.at[0]).wait()


def readout(query_ref, w_ref, out, w_out, out_v, sem):
    copies = [
        pltpu.make_async_copy(w_ref, w_out, sem.at[0]),
        pltpu.make_async_copy(out_v, out, sem.at[1]),
    ]
    copies[0].start()
    D = w_ref.shape[2]
    for h in range(HEADS):
        cols = slice(h * D, (h + 1) * D)
        query = query_ref[:, cols]
        gate = dot(query, w_ref[h, 0])
        upper = dot(query, w_ref[h, 1])
        hidden = (gate * jax.nn.sigmoid(gate) * upper).astype(BF16)
        out_v[:, cols] = dot(hidden, w_ref[h, 2]).astype(BF16)
    copies[1].start()
    for cp in copies:
        cp.wait()


def body(Z, keys, values, queries, rates, fast_weights):
    D = fast_weights.shape[2]
    tokens = keys.shape[0]
    rows = tokens * 4
    vmem = pl.BlockSpec(memory_space=pltpu.VMEM)
    hbm = pl.BlockSpec(memory_space=pltpu.MemorySpace.HBM)

    def run(*refs):
        kernel(Z, *refs)

    query, fresh = pl.pallas_call(
        run,
        out_shape=(
            jax.ShapeDtypeStruct((tokens, HEADS * D), BF16),
            jax.ShapeDtypeStruct((HEADS, 3, D, D), BF16),
        ),
        in_specs=[hbm] * 5,
        out_specs=(pl.BlockSpec(memory_space=pl.ANY), pl.BlockSpec(memory_space=pl.ANY)),
        scratch_shapes=[
            pltpu.VMEM((tokens, HEADS * D), BF16),
            pltpu.VMEM(rates.shape, F32),
            pltpu.VMEM((3, D, D), BF16),
            pltpu.VMEM((HEADS, tokens, D), BF16),
            pltpu.VMEM((rows, D), BF16),
            pltpu.VMEM((rows, D), BF16),
            pltpu.VMEM((2, rows, D), F32),
            pltpu.VMEM((3, rows, D), BF16),
            pltpu.VMEM((3, D, D), F32),
            pltpu.VMEM((3, SUM_CHUNKS, D // SUM_CHUNKS, D), BF16),
            pltpu.VMEM((3, SUM_CHUNKS, D // SUM_CHUNKS, D), BF16),
            pltpu.VMEM((D // SUM_CHUNKS, D), F32),
            pltpu.VMEM((D, D), BF16),
            pltpu.VMEM((D, D), BF16),
            pltpu.VMEM((D, D), BF16),
            pltpu.VMEM((D, D), BF16),
            pltpu.VMEM((HEADS, 3, D, D), BF16),
            pltpu.SemaphoreType.DMA((3,)),
            pltpu.SemaphoreType.DMA((2, 4)),
            pltpu.SemaphoreType.DMA((3,)),
            pltpu.SemaphoreType.DMA((3, SUM_CHUNKS)),
            pltpu.SemaphoreType.DMA((4,)),
            pltpu.SemaphoreType.DMA((2, CHUNKS // 2)),
            pltpu.SemaphoreType.DMA((1,)),
            pltpu.SemaphoreType.DMA((1,)),
            pltpu.SemaphoreType.DMA((5,)),
        ],
        compiler_params=pltpu.CompilerParams(
            collective_id=0, has_side_effects=True, vmem_limit_bytes=30 * 1024 * 1024
        ),
        name="ttt_step",
    )(*[pltpu.with_memory_space_constraint(a, pltpu.MemorySpace.HBM) for a in (keys, values, queries, rates, fast_weights)])
    return pl.pallas_call(
        readout,
        out_shape=(
            jax.ShapeDtypeStruct(query.shape, BF16),
            jax.ShapeDtypeStruct(fresh.shape, BF16),
        ),
        in_specs=[vmem] * 2,
        out_specs=(hbm, hbm),
        scratch_shapes=[
            pltpu.VMEM(query.shape, BF16),
            pltpu.SemaphoreType.DMA((2,)),
        ],
        compiler_params=pltpu.CompilerParams(vmem_limit_bytes=4 * 1024 * 1024),
        name="readout",
    )(query, fresh)


def solution(mesh):
    Z = mesh.shape["tok"] // 4
    return jax.shard_map(
        functools.partial(body, Z),
        mesh=mesh,
        in_specs=(
            P(("grp", "tok"), None),
            P(("grp", "tok"), None),
            P(("grp", "tok"), None),
            P(None, ("grp", "tok")),
            P(),
        ),
        out_specs=(P(("grp", "tok"), None), P("grp", None, None, None)),
        check_vma=False,
    )
```

```python
import functools

import jax
import jax.numpy as jnp
from jax import lax
from jax.experimental import pallas as pl
from jax.experimental.pallas import tpu as pltpu
from jax.sharding import PartitionSpec as P

HEADS = 2
NS_BLOCKS = 8
CHUNKS = 16
SUM_CHUNKS = 16
SUM_LAG = 7
LAG = 5
LEAF = 16
LEAF_END = 8
LATE = 4
SHIFT = 0
MESH = pl.DeviceIdType.MESH
F32 = jnp.float32
BF16 = jnp.bfloat16


def dot(a, b):
    return jnp.dot(a, b, preferred_element_type=F32)


def dot_nt(a, b):
    return lax.dot_general(a, b, (((1,), (1,)), ((), ())), preferred_element_type=F32)


def dot_tn(a, b):
    return lax.dot_general(a, b, (((0,), (0,)), ((), ())), preferred_element_type=F32)


def kernel(
    Z,
    k_hbm, v_hbm, q_hbm, r_hbm, w_hbm,
    query_ref, neww_ref,
    v_ref, r_ref, w_ref,
    o_loc, keys, outer, gates, grads, sums, recv, sendbuf, square, m_buf, x_buf, g_buf, mix_buf, wn,
    tok_send, tok_recv, chain_send, chain_recv, w_send, w_recv, s_recv, out_sem, in_sem,
):
    tokens = k_hbm.shape[0]
    D = w_ref.shape[1]
    R = D // CHUNKS
    S = D // SUM_CHUNKS
    me = lax.axis_index("tok")
    c = me % 2
    y = (me // 2) % 2
    z = me // 4

    def mid(h):
        return Z // 2 - 1 + SHIFT * h

    def at(zz, yy, cc):
        return {"tok": (zz * 2 + yy) * 2 + cc}

    def block_rows(p):
        return pl.ds(pl.multiple_of(p * tokens, tokens), tokens)

    def head_cols(h):
        return pl.ds(pl.multiple_of(h * D, D), D)

    sibling = at(z, y, 1 - c)
    across = at(z, 1 - y, c)
    mine = y * 2 + c
    pair = c == 1
    gatherer = at(z, 1 - y, 1)
    middle = z == mid(y)
    sums_here = jnp.logical_or(pair, middle)

    barrier = pltpu.get_barrier_semaphore()
    for peer in (sibling, across, at(z, 1 - y, 1 - c)):
        pl.semaphore_signal(barrier, inc=1, device_id=peer, device_id_type=MESH)

    @pl.when(z > 0)
    def _():
        pl.semaphore_signal(barrier, inc=1, device_id={"tok": me - 4}, device_id_type=MESH)

    @pl.when(z < Z - 1)
    def _():
        pl.semaphore_signal(barrier, inc=1, device_id={"tok": me + 4}, device_id_type=MESH)

    loads = [
        pltpu.make_async_copy(src, dst, in_sem.at[n])
        for n, (src, dst) in enumerate((
            (r_hbm, r_ref), (v_hbm, v_ref),
            (k_hbm.at[:, head_cols(y)], keys.at[block_rows(mine), :]),
            (w_hbm.at[y], w_ref), (q_hbm, query_ref),
        ))
    ]
    for load in loads:
        load.start()
    square[...] = jnp.zeros_like(square)

    def token_copy(a, kind):
        h = y if kind == 0 else 1 - y
        src = o_loc.at[h] if a else k_hbm.at[:, head_cols(h)]
        return pltpu.make_async_remote_copy(
            src, (keys, outer)[a].at[block_rows(mine), :],
            tok_send.at[kind], tok_recv.at[a, mine],
            device_id=gatherer if kind else sibling, device_id_type=MESH)

    def pass_on(a, p):
        block = (keys, outer)[a].at[block_rows(p), :]
        return pltpu.make_async_remote_copy(
            block, block, tok_send.at[2], tok_recv.at[a, p],
            device_id=sibling, device_id_type=MESH)

    def token_wait(kind):
        block = keys.at[pl.ds(0, tokens * (4 if kind == 2 else 2)), :]
        return pltpu.make_async_remote_copy(
            block, block, tok_send.at[kind], tok_recv.at[0, 0],
            device_id=sibling, device_id_type=MESH)

    def send_tokens(a):
        token_copy(a, 1).start()

        @pl.when(jnp.logical_or(jnp.logical_not(pair), middle))
        def _():
            token_copy(a, 0).start()

    pl.semaphore_wait(barrier, 3 + jnp.where(z > 0, 1, 0) + jnp.where(z < Z - 1, 1, 0))
    send_tokens(0)
    loads[0].wait()
    loads[1].wait()
    for h in range(HEADS):
        row = jnp.broadcast_to(r_ref[h : h + 1, :], (128, tokens))
        col = jnp.concatenate([row.T] * (D // 128), axis=1)
        o_loc[h] = (-col * v_ref[:, h * D : (h + 1) * D].astype(F32)).astype(BF16)

    send_tokens(1)
    outer[block_rows(mine), :] = o_loc[y]
    loads[2].wait()
    loads[3].wait()

    def forward_step(s, _):
        d = s // 4 * 2 + s % 2
        p = jnp.where(d < 2, y * 2 + jnp.where(d == 0, c, 1 - c), (1 - y) * 2 + d % 2)
        rows = block_rows(p)
        for a in range(2):

            @pl.when(jnp.logical_and(s // 2 % 2 == a, d > 0))
            def _():
                pass_on(a, p).wait_recv()

                @pl.when(jnp.logical_and(jnp.logical_and(pair, middle), d >= 2))
                def _():
                    pass_on(a, p).start()

        @pl.when(s // 2 % 2 == 0)
        def _():
            key = keys[rows, :]
            gate = dot(key, w_ref[0])
            upper = dot(key, w_ref[1])

            sigma = jax.nn.sigmoid(gate)
            silu_gate = gate * sigma
            gates[0, rows, :] = upper * sigma * (1.0 + gate * (1.0 - sigma))
            gates[1, rows, :] = silu_gate
            grads[2, rows, :] = (silu_gate * upper).astype(BF16)

        @pl.when(jnp.logical_and(pair, s // 2 % 2 == 1))
        def _():
            back = dot_nt(outer[rows, :], w_ref[2])
            grads[0, rows, :] = (back * gates[0, rows, :]).astype(BF16)
            grads[1, rows, :] = (back * gates[1, rows, :]).astype(BF16)

        return 0

    lax.fori_loop(0, jnp.where(sums_here, 8, 0), forward_step, 0)

    def owner_z(w, h):
        return (0, Z - 1, mid(h))[w]

    def chain_copy(w, i, step, side):
        there = z + step == mid(y)
        held = jnp.where(there, side, 2) if w == 2 else w
        core = jnp.where(there, 0, 1) if w == 2 else 1
        return pltpu.make_async_remote_copy(
            sendbuf.at[w, i], recv.at[held, i], chain_send.at[w], chain_recv.at[held, i],
            device_id=at(z + step, y, core), device_id_type=MESH)

    def chain_sent(w):
        block = sendbuf.at[w]
        return pltpu.make_async_remote_copy(
            block, block, chain_send.at[w], chain_recv.at[w, 0],
            device_id=sibling, device_id_type=MESH)

    def chain_roles(w):
        own = owner_z(w, y)
        return (
            jnp.logical_and(z > 0, z <= own), jnp.logical_and(z < Z - 1, z >= own),
            z == own, z < own, z > own,
        )

    def reduce_event(w, i, roles):
        below, above, ends, rises, falls = roles
        rows = pl.ds(pl.multiple_of(i * S, S), S)

        def take(side):
            held = jnp.where(middle, side, 2) if w == 2 else w
            block = recv.at[held, i]
            pltpu.make_async_remote_copy(
                block, block, chain_send.at[w], chain_recv.at[held, i],
                device_id=sibling, device_id_type=MESH).wait_recv()
            sums[w, rows, :] += recv[held, i].astype(F32)

        @pl.when(below)
        def _():
            take(0)

        @pl.when(above)
        def _():
            take(1)

        @pl.when(ends)
        def _():
            rounded = sums[w, rows, :].astype(BF16)
            m_buf[rows, :] = rounded
            square[...] += jnp.square(rounded.astype(F32))

        @pl.when(jnp.logical_not(ends))
        def _():
            sendbuf[w, i] = sums[w, rows, :].astype(BF16)

        @pl.when(rises)
        def _():
            chain_copy(w, i, 1, 0).start()

        @pl.when(falls)
        def _():
            chain_copy(w, i, -1, 1).start()

    def depth(w):
        own = owner_z(w, y)
        rise = jnp.where(z <= own, z, 0)
        fall = jnp.where(z >= own, Z - 1 - z, 0)
        return SUM_LAG * jnp.maximum(rise, fall)

    def reduce_all(ws, depths, live):
        roles = [chain_roles(w) for w in ws]

        def step(t, _):
            for w, lag, role, on in zip(ws, depths, roles, live):
                i = t - lag

                @pl.when(jnp.logical_and(on, jnp.logical_and(i >= 0, i < SUM_CHUNKS)))
                def _():
                    reduce_event(w, i, role)

            return 0

        return step

    @pl.when(pair)
    def _():
        depths = [depth(0), depth(1), depth(2) + SUM_CHUNKS]
        step = reduce_all((0, 1, 2), depths, (True, True, jnp.logical_not(middle)))
        near = jnp.where(2 * z < Z, 1, 0)
        edge = jnp.logical_or(z == 0, z == Z - 1)
        first = jnp.where(edge, SUM_CHUNKS, 0)

        def near_part(n, _):
            rows = pl.ds(pl.multiple_of(n * (D // 4), D // 4), D // 4)
            sums[near, rows, :] = dot_tn(keys[:, rows], grads[near])
            lax.fori_loop(first * n // 4, first * (n + 1) // 4, step, 0)
            return 0

        lax.fori_loop(0, 4, near_part, 0)
        sums[1 - near] = dot_tn(keys[...], grads[1 - near])
        sums[2] = dot_tn(grads[2], outer[...])
        lax.fori_loop(first, SUM_CHUNKS + functools.reduce(jnp.maximum, depths), step, 0)

    @pl.when(jnp.logical_and(jnp.logical_not(pair), middle))
    def _():
        sums[2] = dot_tn(grads[2], outer[...])
        lax.fori_loop(0, SUM_CHUNKS, reduce_all((2,), (0,), (True,)), 0)

    def owns(w):
        return jnp.logical_and(pair == (w < 2), z == owner_z(w, y))

    def w_targets(w, home):
        own = owner_z(w, y)
        leaf = (2, True, sibling)
        if not home:
            return (leaf,)
        return (
            (3, True, across),
            (0, jnp.logical_and(z >= own, z < Z - 1), {"tok": me + 4}),
            (1, jnp.logical_and(z <= own, z > (1 if w == 1 else 0)), {"tok": me - 4}),
            leaf,
        )

    def arrival(w, leaf, i):
        return w_recv.at[w % 2, i // 2] if leaf else chain_recv.at[w % 2, i]

    def w_copies(h, w, i, targets, size=1):
        rows = pl.ds(pl.multiple_of(i * R, R), size * R)
        block = wn.at[h, w, rows, :]

        def copy(kind, dev):
            pltpu.make_async_remote_copy(
                block, block, w_send.at[kind],
                arrival(w, kind == 3, i) if kind != 2 else s_recv.at[0],
                device_id=dev, device_id_type=MESH).start()

        for kind, go, dev in targets:
            if go is True:
                copy(kind, dev)
            else:

                @pl.when(go)
                def _():
                    copy(kind, dev)

    def w_wait(block, kind):
        return pltpu.make_async_remote_copy(
            block, block, w_send.at[kind], s_recv.at[0],
            device_id=sibling, device_id_type=MESH)

    def wait_block(h, w, i, leaf, size):
        rows = pl.ds(pl.multiple_of(i * R, R), size * R)
        block = wn.at[h, w, rows, :]
        pltpu.make_async_remote_copy(
            block, block, w_send.at[2], arrival(w, leaf, i),
            device_id=sibling, device_id_type=MESH).wait_recv()

    is_owner = functools.reduce(jnp.logical_or, [owns(w) for w in range(3)])
    owned_w = jnp.where(owns(0), 0, jnp.where(owns(1), 1, 2))

    def renew(i, targets):
        rows = slice(i * R, (i + 1) * R)
        old = w_ref[owned_w, rows, :].astype(F32)
        fresh = old - m_buf[rows, :].astype(F32)
        scale = jnp.sqrt(
            (jnp.mean(old * old, axis=1, keepdims=True) + 1e-06)
            / (jnp.mean(fresh * fresh, axis=1, keepdims=True) + 1e-06)
        )
        wn[y, owned_w, rows, :] = (fresh * scale).astype(BF16)
        w_copies(y, owned_w, i, targets)

    @pl.when(is_owner)
    def _():
        scale = 1.0 / (jnp.sqrt(jnp.sum(square[...])) + 1e-07)

        def mix(x_ref, factor):
            x = x_ref[...]
            g_buf[...] = (dot_nt(x, x) * factor).astype(BF16)
            g = g_buf[...]
            mix_buf[...] = (-4.775 * g.astype(F32) + 2.0315 * dot(g, g)).astype(BF16)

        mix(m_buf, scale * scale)
        m = m_buf[...]
        x_buf[...] = ((3.4445 * m.astype(F32) + dot(mix_buf[...], m)) * scale).astype(BF16)
        mix(x_buf, 1.0)
        edges = (
            (3, True, across), (0, z < Z - 1, {"tok": me + 4}),
            (1, z > 0, {"tok": me - 4}), (2, True, sibling),
        )
        step_rows = D // NS_BLOCKS
        for b in range(NS_BLOCKS):
            wide = slice(b * step_rows, (b + 1) * step_rows)
            m_buf[wide, :] = (
                3.4445 * x_buf[wide, :].astype(F32) + dot(mix_buf[wide, :], x_buf[...])
            ).astype(BF16)
            for i in range(b * CHUNKS // NS_BLOCKS, (b + 1) * CHUNKS // NS_BLOCKS):
                renew(i, edges)

    def spread_all(ws):
        routes = []
        end = 0
        for home in (True, False):
            h = y if home else 1 - y
            for w in ws:
                away = jnp.abs(z - owner_z(w, h))
                hops = away + (0 if home else 1)
                edge = jnp.logical_or(z == 0, z == Z - 1)
                start = LAG * jnp.maximum(away - 1, 0)
                if not home:
                    start = start + jnp.where(away > 0, jnp.where(edge, LEAF_END, LEAF), 0)
                routes.append((h, w, start, hops > 0, True, w_targets(w, home), not home))
                end = jnp.maximum(end, start + CHUNKS)
                if home and w == 1:
                    down = [(1, True, {"tok": me - 4})]
                    routes.append((h, w, start + LATE, z == 1, False, down, False))
                    end = jnp.maximum(end, start + LATE + CHUNKS)

        def step(t, _):
            for h, w, start, live, waits, targets, leaf in routes:
                i = t - start
                due = jnp.logical_and(i >= 0, i < CHUNKS)
                if leaf:
                    due = jnp.logical_and(due, i % 2 == 1)
                size = 2 if leaf else 1

                @pl.when(jnp.logical_and(live, due))
                def _():
                    if waits:
                        wait_block(h, w, i - (size - 1), leaf, size)
                    w_copies(h, w, i - (size - 1), targets, size)

            return 0

        lax.fori_loop(0, end, step, 0)

    @pl.when(pair)
    def _():
        spread_all((0, 1))

    @pl.when(jnp.logical_not(pair))
    def _():
        spread_all((2,))

    def save(h, w):
        return pltpu.make_async_copy(wn.at[h, w], neww_ref.at[h, w], out_sem.at[0])

    def save_all(ws):
        for w in ws:
            for h in range(HEADS):
                save(h, w).start()

    def finish(own, others):
        save_all(own)
        w_wait(wn.at[:, others[0] : others[-1] + 1], 2).wait_recv()
        save_all(others)

    @pl.when(pair)
    def _():
        finish((0, 1), (2,))

    @pl.when(jnp.logical_not(pair))
    def _():
        finish((2,), (0, 1))

    loads[4].wait()

    token_wait(1).wait_send()

    @pl.when(jnp.logical_or(jnp.logical_not(pair), middle))
    def _():
        token_wait(0).wait_send()

    @pl.when(jnp.logical_and(pair, middle))
    def _():
        token_wait(2).wait_send()

    for w in range(3):

        @pl.when(jnp.logical_and(pair, z != owner_z(w, y)))
        def _():
            chain_sent(w).wait_send()

    rise = jnp.where(pair, z < Z - 1, jnp.logical_and(z >= mid(y), z < Z - 1))
    fall = jnp.where(pair, z > 0, jnp.logical_and(z <= mid(y), z > 0))

    @pl.when(rise)
    def _():
        w_wait(wn.at[0, 0], 0).wait_send()

    @pl.when(fall)
    def _():
        w_wait(wn.at[0, 0], 1).wait_send()

    @pl.when(pair)
    def _():
        w_wait(wn.at[0, 0:2], 3).wait_send()
        w_wait(wn.at[:, 0:2], 2).wait_send()

    @pl.when(jnp.logical_not(pair))
    def _():
        w_wait(wn.at[0, 2], 3).wait_send()
        w_wait(wn.at[:, 2:3], 2).wait_send()

    pltpu.make_async_copy(wn, neww_ref, out_sem.at[0]).wait()


def readout(query_ref, w_ref, out, w_out, out_v, sem):
    copies = [
        pltpu.make_async_copy(w_ref, w_out, sem.at[0]),
        pltpu.make_async_copy(out_v, out, sem.at[1]),
    ]
    copies[0].start()
    D = w_ref.shape[2]
    for h in range(HEADS):
        cols = slice(h * D, (h + 1) * D)
        query = query_ref[:, cols]
        gate = dot(query, w_ref[h, 0])
        upper = dot(query, w_ref[h, 1])
        hidden = (gate * jax.nn.sigmoid(gate) * upper).astype(BF16)
        out_v[:, cols] = dot(hidden, w_ref[h, 2]).astype(BF16)
    copies[1].start()
    for cp in copies:
        cp.wait()


def body(Z, keys, values, queries, rates, fast_weights):
    D = fast_weights.shape[2]
    tokens = keys.shape[0]
    rows = tokens * 4
    vmem = pl.BlockSpec(memory_space=pltpu.VMEM)
    hbm = pl.BlockSpec(memory_space=pltpu.MemorySpace.HBM)

    def run(*refs):
        kernel(Z, *refs)

    query, fresh = pl.pallas_call(
        run,
        out_shape=(
            jax.ShapeDtypeStruct((tokens, HEADS * D), BF16),
            jax.ShapeDtypeStruct((HEADS, 3, D, D), BF16),
        ),
        in_specs=[hbm] * 5,
        out_specs=(pl.BlockSpec(memory_space=pl.ANY), pl.BlockSpec(memory_space=pl.ANY)),
        scratch_shapes=[
            pltpu.VMEM((tokens, HEADS * D), BF16),
            pltpu.VMEM(rates.shape, F32),
            pltpu.VMEM((3, D, D), BF16),
            pltpu.VMEM((HEADS, tokens, D), BF16),
            pltpu.VMEM((rows, D), BF16),
            pltpu.VMEM((rows, D), BF16),
            pltpu.VMEM((2, rows, D), F32),
            pltpu.VMEM((3, rows, D), BF16),
            pltpu.VMEM((3, D, D), F32),
            pltpu.VMEM((3, SUM_CHUNKS, D // SUM_CHUNKS, D), BF16),
            pltpu.VMEM((3, SUM_CHUNKS, D // SUM_CHUNKS, D), BF16),
            pltpu.VMEM((D // SUM_CHUNKS, D), F32),
            pltpu.VMEM((D, D), BF16),
            pltpu.VMEM((D, D), BF16),
            pltpu.VMEM((D, D), BF16),
            pltpu.VMEM((D, D), BF16),
            pltpu.VMEM((HEADS, 3, D, D), BF16),
            pltpu.SemaphoreType.DMA((3,)),
            pltpu.SemaphoreType.DMA((2, 4)),
            pltpu.SemaphoreType.DMA((3,)),
            pltpu.SemaphoreType.DMA((3, SUM_CHUNKS)),
            pltpu.SemaphoreType.DMA((4,)),
            pltpu.SemaphoreType.DMA((2, CHUNKS // 2)),
            pltpu.SemaphoreType.DMA((1,)),
            pltpu.SemaphoreType.DMA((1,)),
            pltpu.SemaphoreType.DMA((5,)),
        ],
        compiler_params=pltpu.CompilerParams(
            collective_id=0, has_side_effects=True, vmem_limit_bytes=30 * 1024 * 1024
        ),
        name="ttt_step",
    )(*[pltpu.with_memory_space_constraint(a, pltpu.MemorySpace.HBM) for a in (keys, values, queries, rates, fast_weights)])
    return pl.pallas_call(
        readout,
        out_shape=(
            jax.ShapeDtypeStruct(query.shape, BF16),
            jax.ShapeDtypeStruct(fresh.shape, BF16),
        ),
        in_specs=[vmem] * 2,
        out_specs=(hbm, hbm),
        scratch_shapes=[
            pltpu.VMEM(query.shape, BF16),
            pltpu.SemaphoreType.DMA((2,)),
        ],
        compiler_params=pltpu.CompilerParams(vmem_limit_bytes=4 * 1024 * 1024),
        name="readout",
    )(query, fresh)


def solution(mesh):
    Z = mesh.shape["tok"] // 4
    return jax.shard_map(
        functools.partial(body, Z),
        mesh=mesh,
        in_specs=(
            P(("grp", "tok"), None),
            P(("grp", "tok"), None),
            P(("grp", "tok"), None),
            P(None, ("grp", "tok")),
            P(),
        ),
        out_specs=(P(("grp", "tok"), None), P("grp", None, None, None)),
        check_vma=False,
    )
```
